32 devices in a mesh: tgt: 4 (over y, x), sup: 8 (over z, core).
Axes of the slice: x: 2, y: 2, z: 4, core: 2. Of those that a mesh axis runs over, the one named last changes fastest.
Arguments:
- support: float32 [32, 3, 1024], P(('sup', 'tgt')), may hold values from -14 to 14
- coeffs: float32 [32, 100], P('sup'), may hold values from -10 to 10
- targets: float32 [32, 3, 1024], P(('tgt', 'sup')), may hold values from -14 to 14
- labels: float32 [32, 100], P(('tgt', 'sup')), may hold values from -5 to 5
Outputs:
- support_grad: float32 [32, 3, 1024], P(('sup', 'tgt'))
- residual: float32 [32, 100], P(('tgt', 'sup'))
The draws below stay inside these ranges and needn't reach their ends.
All inputs are finite; a program needn't handle non-finite values.
Results may differ from the reference program's by a relative error of at most 0.000064.
Values sent between devices are 32-bit elements; how exact they have to be, the bound alone decides.
No kernel may reach another device: no remote copies, remote signals or barrier semaphores. Data moves between devices by JAX's collectives and lax.ppermute only.
A program may use at most 128 MiB of HBM per device.

```python
import math
import jax
import jax.numpy as jnp
from jax import lax

SIDE = 32
CH = 3
LABELS = 100
DEPTH = 3
SUP_DEV = 1
PIX = 1024
SUPPORTS = 32
TARGETS = 32
N_TGT = 4


prototype_count = 16


def prototype_bank(key):
    return jax.random.truncated_normal(jax.random.fold_in(key, 9001), -3.0, 3.0, (prototype_count, CH, PIX), jnp.float32)


def class_signs(key, image_count, salt_value):
    classes = jax.random.randint(jax.random.fold_in(key, salt_value), (image_count,), 0, prototype_count)
    sign_values = 2 * jax.random.randint(jax.random.fold_in(key, salt_value + 1), (image_count,), 0, 2) - 1
    return (classes, sign_values)


def mixed_images(key, image_count, salt_value):
    classes, sign_values = class_signs(key, image_count, salt_value)
    proto_bank = prototype_bank(key)
    amplitude = jax.random.uniform(jax.random.fold_in(key, salt_value + 2), (image_count,), jnp.float32, 0.7, 1.3)
    amplitude = amplitude * sign_values.astype(jnp.float32)
    noise_key = jax.random.fold_in(key, salt_value + 3)
    noise_part = jax.random.truncated_normal(noise_key, -3.0, 3.0, (image_count, CH, PIX), jnp.float32)
    images = amplitude[:, None, None] * jnp.take(proto_bank, classes, axis=0) + noise_part
    return images


def draw_support(key, part):
    return mixed_images(key, SUPPORTS, 101)


def draw_targets(key, part):
    return mixed_images(key, TARGETS, 201)


def draw_coeffs(key, part):
    classes, sign_values = class_signs(key, SUPPORTS, 101)
    pattern = jax.random.normal(jax.random.fold_in(key, 9002), (prototype_count, LABELS), jnp.float32)
    noise_key = jax.random.fold_in(key, 9003)
    noise_part = jax.random.normal(noise_key, (SUPPORTS, LABELS), jnp.float32)
    raw_coeffs = sign_values.astype(jnp.float32)[:, None] * jnp.take(pattern, classes, axis=0) + noise_part
    return 80.0 / SUPPORTS * jnp.clip(raw_coeffs, -4.0, 4.0)


def shard_levels(own_key, dims, cuts, low, high):
    def one(position, parts):
        steps = jax.random.uniform(jax.random.fold_in(jax.random.fold_in(own_key, 6), position), (parts,), jnp.float32, low / len(cuts), high / len(cuts))
        return jnp.repeat(jnp.exp(steps), dims[position] // parts).reshape((-1,) + (1,) * (len(dims) - position - 1))

    loudness = one(*cuts[0])
    for cut in cuts[1:]:
        loudness = loudness * one(*cut)
    return loudness


def normal_values(key, dims, scale, bound, split=(), held_as=jnp.bfloat16):
    result = jax.random.normal(key, dims, jnp.float32) * scale
    if len(split) > 0:
        result = shard_levels(key, dims, split, -0.22, 0.18) * result
    return jnp.clip(result, min=-bound, max=bound).astype(held_as)


def setup_inputs(seed: int = 0) -> dict:
    key_of = jax.random.split(jax.random.key(seed), 5)
    return {
        "support": draw_support(jax.random.fold_in(key_of[4], 71), 0),
        "coeffs": draw_coeffs(jax.random.fold_in(key_of[4], 71), 0),
        "targets": draw_targets(jax.random.fold_in(key_of[4], 71), 0),
        "labels": normal_values(key_of[3], (TARGETS, LABELS), 1.0, 5.0, ((0, 32),), jnp.float32),
    }


WEIGHT_VAR = 1.6
BIAS_VAR = 0.1

def spread(values):
    side_cells = values.shape[0]
    padded = jnp.pad(values, ((1, 1), (1, 1), (0, 0)))
    summed = jnp.zeros_like(values)
    for row_shift in range(3):
        for col_shift in range(3):
            summed = summed + padded[row_shift:row_shift + side_cells, col_shift:col_shift + side_cells]
    return summed / 9.0

def self_levels(images):
    image_count = images.shape[0]
    energy = lax.optimization_barrier(jnp.mean(images * images, axis=1))
    kernel_level = WEIGHT_VAR * spread(energy.T.reshape(SIDE, SIDE, image_count)) + BIAS_VAR
    levels = [kernel_level]
    for layer_idx in range(DEPTH - 1):
        activated = 2.0 / math.pi * jnp.arcsin(2.0 * kernel_level / (1.0 + 2.0 * kernel_level))
        kernel_level = WEIGHT_VAR * spread(activated) + BIAS_VAR
        levels.append(kernel_level)
    return levels

def pair_kernel(support, targets):
    sup_count = support.shape[0]
    tgt_count = targets.shape[0]
    sup_levels = self_levels(support)
    tgt_levels = self_levels(targets)
    products = jnp.einsum('scp,tcp->pst', support, targets, precision=lax.Precision.HIGHEST) / support.shape[1]
    kernel_level = WEIGHT_VAR * spread(products.reshape(SIDE, SIDE, sup_count * tgt_count)) + BIAS_VAR
    activated = kernel_level
    for layer_idx in range(DEPTH):
        sup_gain = lax.rsqrt(1.0 + 2.0 * sup_levels[layer_idx])
        tgt_gain = lax.rsqrt(1.0 + 2.0 * tgt_levels[layer_idx])
        correlation = 2.0 * kernel_level.reshape(SIDE, SIDE, sup_count, tgt_count) * sup_gain[:, :, :, None] * tgt_gain[:, :, None, :]
        activated = 2.0 / math.pi * jnp.arcsin(correlation)
        if layer_idx + 1 < DEPTH:
            kernel_level = WEIGHT_VAR * spread(activated.reshape(SIDE, SIDE, sup_count * tgt_count)) + BIAS_VAR
    return WEIGHT_VAR * lax.optimization_barrier(jnp.mean(activated, axis=(0, 1))) + BIAS_VAR

def reference(support, coeffs, targets, labels):
    block_size = SUP_DEV * N_TGT
    block_count = SUPPORTS // block_size
    blocks = support.reshape(block_count, block_size, CH, PIX)
    coeff_blocks = coeffs.reshape(block_count, block_size, LABELS)

    def block_predict(pair):
        piece, block_coeffs = pair
        theta = pair_kernel(piece, targets)
        return jnp.dot(theta.T, block_coeffs, precision=lax.Precision.HIGHEST, preferred_element_type=jnp.float32)
    predicted = lax.optimization_barrier(jnp.sum(lax.map(block_predict, (blocks, coeff_blocks)), axis=0))
    misfit = predicted - labels

    def block_gradient(pair):
        piece, block_coeffs = pair
        theta, pullback = jax.vjp(lambda images: pair_kernel(images, targets), piece)
        cotangent = jnp.dot(block_coeffs, misfit.T, precision=lax.Precision.HIGHEST, preferred_element_type=jnp.float32)
        return pullback(cotangent)[0]
    gradients = lax.map(block_gradient, (blocks, coeff_blocks))
    return (gradients.reshape(SUPPORTS, CH, PIX), misfit)
```

```python
import functools
import math

import jax
import jax.numpy as jnp
from jax import lax
from jax.experimental import pallas as pl
from jax.experimental.pallas import tpu as pltpu
from jax.sharding import Mesh
from jax.sharding import PartitionSpec as P

WEIGHT_VAR = 1.6
BIAS_VAR = 0.1
CH = 3
SUB = 8
LANE = 128
TWO_PI = 2.0 / math.pi
CHUNK = 8


def arcsine(x):
    a = jnp.abs(x)
    large = a > 0.5
    z = jnp.where(large, 0.5 - 0.5 * a, a * a)
    y = jnp.where(large, jnp.sqrt(z), a)
    p = 4.2163199048e-2 * z + 2.4181311049e-2
    p = p * z + 4.5470025998e-2
    p = p * z + 7.4953002686e-2
    p = p * z + 1.6666752422e-1
    y = p * z * y + y
    y = jnp.where(large, (0.5 * math.pi) - 2.0 * y, y)
    return jnp.where(x < 0.0, -y, y)


def box_sum(side):
    lane = lax.broadcasted_iota(jnp.int32, (SUB, LANE), 1)
    sub = lax.broadcasted_iota(jnp.int32, (SUB, LANE), 0)
    column = lane % side
    not_left, not_right = column != 0, column != side - 1
    inner_up, inner_down = lane >= side, lane < LANE - side
    not_top, not_bottom = sub != 0, sub != SUB - 1

    def apply(x):
        lanes, subs = x.ndim - 1, x.ndim - 2
        h = (
            x
            + jnp.where(not_left, pltpu.roll(x, 1, lanes), 0.0)
            + jnp.where(not_right, pltpu.roll(x, LANE - 1, lanes), 0.0)
        )
        above = pltpu.roll(h, side, lanes)
        below = pltpu.roll(h, LANE - side, lanes)
        above = jnp.where(
            inner_up, above, jnp.where(not_top, pltpu.roll(above, 1, subs), 0.0)
        )
        below = jnp.where(
            inner_down, below, jnp.where(not_bottom, pltpu.roll(below, SUB - 1, subs), 0.0)
        )
        return h + above + below

    return apply


def self_levels(images, box):
    energy = sum(image * image for image in images)
    level = (WEIGHT_VAR / (9 * CH)) * box(energy) + BIAS_VAR
    levels, gains = [], []
    for layer in range(3):
        gain = lax.rsqrt(1.0 + 2.0 * level)
        levels.append(level)
        gains.append(gain)
        if layer < 2:
            level = (WEIGHT_VAR * TWO_PI / 9) * box(
                arcsine(2.0 * level / (1.0 + 2.0 * level))
            ) + BIAS_VAR
    return levels, gains


def channels(ref, *lead):
    return [ref[lead + (slice(c * SUB, (c + 1) * SUB), slice(None))] for c in range(CH)]


def pair_body(side, pixels, row_of, own_ref, oth_ref, sup_ref, coef_ref, lab_ref, row_ref, plane_ref, level_ref, sums):
    half = own_ref.shape[0]
    box = box_sum(side)
    core = lax.axis_index("core")
    support = channels(sup_ref)
    sup_levels, sup_gains = self_levels(support, box)
    for layer in range(3):
        level_ref[layer] = sup_levels[layer]
    sup_gains = [2.0 * gain for gain in sup_gains]

    def step(image_ref, base, i):
        at = pl.ds(i * CHUNK, CHUNK)
        target = channels(image_ref, at)
        _, tgt_gains = self_levels(target, box)
        level = (WEIGHT_VAR / (9 * CH)) * box(
            sum(s * t for s, t in zip(support, target))
        ) + BIAS_VAR
        gains, corrs = [], []
        for layer in range(3):
            gain = sup_gains[layer] * tgt_gains[layer]
            corr = level * gain
            gains.append(gain)
            corrs.append(corr)
            angle = arcsine(corr)
            if layer < 2:
                level = (WEIGHT_VAR * TWO_PI / 9) * box(angle) + BIAS_VAR
        to = pl.ds(base + i * CHUNK, CHUNK)
        sums[to] = jnp.sum(angle, axis=1)
        grad = (WEIGHT_VAR * TWO_PI / pixels)
        for layer in (2, 1, 0):
            corr = corrs[layer]
            slope = grad * lax.rsqrt((1.0 - corr) * (1.0 + corr))
            plane_ref[to, 1 + layer] = slope * corr
            spread = box(slope * gains[layer])
            if layer > 0:
                grad = (WEIGHT_VAR * TWO_PI / 9) * spread
            else:
                plane_ref[to, 0] = (WEIGHT_VAR / (9 * CH)) * spread

    def both(i, carry):
        step(own_ref, core * half, i)
        step(oth_ref, (1 - core) * half, i)
        return carry

    lax.fori_loop(0, half // CHUNK, both, 0)
    width = row_of["theta"]
    total = lax.dot_general(
        jnp.ones((SUB, LANE), jnp.float32),
        sums[...],
        (((1,), (1,)), ((), ())),
        precision=lax.Precision.HIGHEST,
        preferred_element_type=jnp.float32,
    )
    row_ref[...] = jnp.zeros_like(row_ref)
    row_ref[0:1, 0 : 2 * half] = (WEIGHT_VAR * TWO_PI / pixels) * total[0:1] + BIAS_VAR
    labels = lab_ref.shape[-1]
    own = lax.axis_index("tgt")
    row_ref[0:1, width : width + labels] = coef_ref[pl.ds(own, 1), :]
    row_ref[0:1, width + row_of["class"] : width + row_of["class"] + labels] = lab_ref[...]


def final_body(side, row_of, index_of, all_ref, own_ref, oth_ref, sup_ref, plane_ref, level_ref, grad_ref, res_ref, weight, misfits):
    half = own_ref.shape[0]
    box = box_sum(side)
    core = lax.axis_index("core")
    me = index_of()
    width, classes = row_of["theta"], row_of["class"]
    theta = all_ref[:, 0, 0 : 2 * half]
    coeffs = all_ref[:, 0, width : width + classes]
    labels = all_ref[:, 0, width + classes : width + 2 * classes]
    misfit = (
        lax.dot_general(
            theta,
            coeffs,
            (((0,), (0,)), ((), ())),
            precision=lax.Precision.HIGHEST,
            preferred_element_type=jnp.float32,
        )
        - labels
    )
    own_coeffs = all_ref[me, :, width : width + classes]
    cot = jnp.sum(misfit * own_coeffs, axis=1, keepdims=True)
    misfits[...] = misfit
    res_ref[...] = misfits[pl.ds(me, 1), 0 : res_ref.shape[-1]]
    weight[...] = jnp.broadcast_to(cot, weight.shape)

    def step(image_ref, base, i, carry):
        acc = list(carry)
        for k in range(CHUNK):
            to = base + i * CHUNK + k
            c = weight[pl.ds(to, SUB, stride=0), :]
            target = channels(image_ref, i * CHUNK + k)
            u = c * plane_ref[to, 0]
            for ch in range(CH):
                acc[ch] = acc[ch] + u * target[ch]
            for layer in range(3):
                acc[CH + layer] = acc[CH + layer] + c * plane_ref[to, 1 + layer]
        return tuple(acc)

    def both(i, carry):
        carry = step(own_ref, core * half, i, carry)
        return step(oth_ref, (1 - core) * half, i, carry)

    zero = jnp.zeros((SUB, LANE), jnp.float32)
    acc = lax.fori_loop(0, half // CHUNK, both, (zero,) * (CH + 3))
    carried = None
    for layer in (2, 1, 0):
        level = level_ref[layer]
        inverse = 1.0 / (1.0 + 2.0 * level)
        direct = -inverse * acc[CH + layer]
        if carried is None:
            carried = direct
        else:
            slope = (2.0 * TWO_PI) * inverse * lax.rsqrt(1.0 + 4.0 * level)
            carried = direct + slope * ((WEIGHT_VAR / 9) * box(carried))
    energy = (2.0 * WEIGHT_VAR / (9 * CH)) * box(carried)
    support = channels(sup_ref)
    for ch in range(CH):
        grad = acc[ch] + energy * support[ch]
        for k in range(SUB):
            grad_ref[0, ch : ch + 1, k * LANE : (k + 1) * LANE] = grad[k : k + 1, :]


def local(support, coeffs, targets, labels):
    f32 = jnp.float32
    pixels = support.shape[2]
    side = math.isqrt(pixels)
    chips = lax.axis_size("tgt") * lax.axis_size("row")
    count = 2 * chips
    classes = pl.cdiv(labels.shape[1], LANE) * LANE
    row_of = {"theta": pl.cdiv(count, LANE) * LANE, "class": classes}
    width = row_of["theta"] + 2 * classes

    image = targets.reshape(CH * SUB, LANE)
    own = lax.all_to_all(
        jnp.broadcast_to(image, (chips,) + image.shape), ("tgt", "row"), 0, 0, tiled=True
    )
    oth = lax.ppermute(own, "core", [(0, 1), (1, 0)])
    sup = support.reshape(CH * SUB, LANE)

    row, planes, levels = pl.pallas_call(
        functools.partial(pair_body, side, pixels, row_of),
        out_shape=(
            jax.ShapeDtypeStruct((1, width), f32),
            jax.ShapeDtypeStruct((count, 4, SUB, LANE), f32),
            jax.ShapeDtypeStruct((3, SUB, LANE), f32),
        ),
        scratch_shapes=[pltpu.VMEM((count, LANE), f32)],
        name="pairs",
    )(own, oth, sup, coeffs, labels)

    rows = lax.all_to_all(
        jnp.broadcast_to(row[None], (count, 1, width)), ("core", "tgt", "row"), 0, 0, tiled=True
    )

    def index_of():
        tgt, rows_, core = (lax.axis_index(a) for a in ("tgt", "row", "core"))
        return (core * lax.axis_size("tgt") + tgt) * lax.axis_size("row") + rows_

    grad, residual = pl.pallas_call(
        functools.partial(final_body, side, row_of, index_of),
        out_shape=(
            jax.ShapeDtypeStruct(support.shape, f32),
            jax.ShapeDtypeStruct(labels.shape, f32),
        ),
        scratch_shapes=[pltpu.VMEM((count, LANE), f32), pltpu.VMEM((count, classes), f32)],
        name="final",
    )(rows, own, oth, sup, planes, levels)
    return grad, residual


def solution(mesh):
    tgt, sup = mesh.devices.shape
    chips = Mesh(mesh.devices.reshape(tgt, sup // 2, 2), ("tgt", "row", "core"))
    by_support, by_target = ("row", "core", "tgt"), ("tgt", "row", "core")
    return jax.shard_map(
        local,
        mesh=chips,
        in_specs=(
            P(by_support, None, None),
            P(("row", "core"), None),
            P(by_target, None, None),
            P(by_target, None),
        ),
        out_specs=(P(by_support, None, None), P(by_target, None)),
        check_vma=False,
    )
```

```python
import functools
import math

import jax
import jax.numpy as jnp
from jax import lax
from jax.experimental import pallas as pl
from jax.experimental.pallas import tpu as pltpu
from jax.sharding import Mesh
from jax.sharding import PartitionSpec as P

WEIGHT_VAR = 1.6
BIAS_VAR = 0.1
CH = 3
SUB = 8
LANE = 128
TWO_PI = 2.0 / math.pi
CHUNK = 8


def arcsine(x):
    a = jnp.abs(x)
    large = a > 0.5
    z = jnp.where(large, 0.5 - 0.5 * a, a * a)
    y = jnp.where(large, jnp.sqrt(z), a)
    p = 4.2163199048e-2 * z + 2.4181311049e-2
    p = p * z + 4.5470025998e-2
    p = p * z + 7.4953002686e-2
    p = p * z + 1.6666752422e-1
    y = p * z * y + y
    y = jnp.where(large, (0.5 * math.pi) - 2.0 * y, y)
    return jnp.where(x < 0.0, -y, y)


def box_sum(side):
    lane = lax.broadcasted_iota(jnp.int32, (SUB, LANE), 1)
    sub = lax.broadcasted_iota(jnp.int32, (SUB, LANE), 0)
    column = lane % side
    not_left, not_right = column != 0, column != side - 1
    inner_up, inner_down = lane >= side, lane < LANE - side
    not_top, not_bottom = sub != 0, sub != SUB - 1

    def apply(x):
        lanes, subs = x.ndim - 1, x.ndim - 2
        h = (
            x
            + jnp.where(not_left, pltpu.roll(x, 1, lanes), 0.0)
            + jnp.where(not_right, pltpu.roll(x, LANE - 1, lanes), 0.0)
        )
        above = pltpu.roll(h, side, lanes)
        below = pltpu.roll(h, LANE - side, lanes)
        above = jnp.where(
            inner_up, above, jnp.where(not_top, pltpu.roll(above, 1, subs), 0.0)
        )
        below = jnp.where(
            inner_down, below, jnp.where(not_bottom, pltpu.roll(below, SUB - 1, subs), 0.0)
        )
        return h + above + below

    return apply


def self_levels(images, box):
    energy = sum(image * image for image in images)
    level = (WEIGHT_VAR / (9 * CH)) * box(energy) + BIAS_VAR
    levels, gains = [], []
    for layer in range(3):
        gain = lax.rsqrt(1.0 + 2.0 * level)
        levels.append(level)
        gains.append(gain)
        if layer < 2:
            level = (WEIGHT_VAR * TWO_PI / 9) * box(
                arcsine(2.0 * level / (1.0 + 2.0 * level))
            ) + BIAS_VAR
    return levels, gains


def channels(ref, *lead):
    return [ref[lead + (slice(c * SUB, (c + 1) * SUB), slice(None))] for c in range(CH)]


def pair_body(side, pixels, row_of, own_ref, oth_ref, sup_ref, coef_ref, lab_ref, row_ref, plane_ref, level_ref, sums):
    half = own_ref.shape[0]
    box = box_sum(side)
    core = lax.axis_index("core")
    support = channels(sup_ref)
    sup_levels, sup_gains = self_levels(support, box)
    for layer in range(3):
        level_ref[layer] = sup_levels[layer]
    sup_gains = [2.0 * gain for gain in sup_gains]

    def step(image_ref, base, i):
        at = pl.ds(i * CHUNK, CHUNK)
        target = channels(image_ref, at)
        _, tgt_gains = self_levels(target, box)
        level = (WEIGHT_VAR / (9 * CH)) * box(
            sum(s * t for s, t in zip(support, target))
        ) + BIAS_VAR
        gains, corrs = [], []
        for layer in range(3):
            gain = sup_gains[layer] * tgt_gains[layer]
            corr = level * gain
            gains.append(gain)
            corrs.append(corr)
            angle = arcsine(corr)
            if layer < 2:
                level = (WEIGHT_VAR * TWO_PI / 9) * box(angle) + BIAS_VAR
        to = pl.ds(base + i * CHUNK, CHUNK)
        sums[to] = jnp.sum(angle, axis=1)
        grad = (WEIGHT_VAR * TWO_PI / pixels)
        for layer in (2, 1, 0):
            corr = corrs[layer]
            slope = grad * lax.rsqrt((1.0 - corr) * (1.0 + corr))
            plane_ref[to, 1 + layer] = slope * corr
            spread = box(slope * gains[layer])
            if layer > 0:
                grad = (WEIGHT_VAR * TWO_PI / 9) * spread
            else:
                plane_ref[to, 0] = (WEIGHT_VAR / (9 * CH)) * spread

    def both(i, carry):
        step(own_ref, core * half, i)
        step(oth_ref, (1 - core) * half, i)
        return carry

    lax.fori_loop(0, half // CHUNK, both, 0)
    width = row_of["theta"]
    total = lax.dot_general(
        jnp.ones((SUB, LANE), jnp.float32),
        sums[...],
        (((1,), (1,)), ((), ())),
        precision=lax.Precision.HIGHEST,
        preferred_element_type=jnp.float32,
    )
    row_ref[...] = jnp.zeros_like(row_ref)
    row_ref[0:1, 0 : 2 * half] = (WEIGHT_VAR * TWO_PI / pixels) * total[0:1] + BIAS_VAR
    labels = lab_ref.shape[-1]
    own = lax.axis_index("tgt")
    row_ref[0:1, width : width + labels] = coef_ref[pl.ds(own, 1), :]
    row_ref[0:1, width + row_of["class"] : width + row_of["class"] + labels] = lab_ref[...]


def final_body(side, row_of, index_of, all_ref, own_ref, oth_ref, sup_ref, plane_ref, level_ref, grad_ref, res_ref, weight, misfits):
    half = own_ref.shape[0]
    box = box_sum(side)
    core = lax.axis_index("core")
    me = index_of()
    width, classes = row_of["theta"], row_of["class"]
    theta = all_ref[:, 0, 0 : 2 * half]
    coeffs = all_ref[:, 0, width : width + classes]
    labels = all_ref[:, 0, width + classes : width + 2 * classes]
    misfit = (
        lax.dot_general(
            theta,
            coeffs,
            (((0,), (0,)), ((), ())),
            precision=lax.Precision.HIGHEST,
            preferred_element_type=jnp.float32,
        )
        - labels
    )
    own_coeffs = all_ref[me, :, width : width + classes]
    cot = jnp.sum(misfit * own_coeffs, axis=1, keepdims=True)
    misfits[...] = misfit
    res_ref[...] = misfits[pl.ds(me, 1), 0 : res_ref.shape[-1]]
    weight[...] = jnp.broadcast_to(cot, weight.shape)

    def step(image_ref, base, i, carry):
        acc = list(carry)
        for k in range(CHUNK):
            to = base + i * CHUNK + k
            c = weight[pl.ds(to, SUB, stride=0), :]
            target = channels(image_ref, i * CHUNK + k)
            u = c * plane_ref[to, 0]
            for ch in range(CH):
                acc[ch] = acc[ch] + u * target[ch]
            for layer in range(3):
                acc[CH + layer] = acc[CH + layer] + c * plane_ref[to, 1 + layer]
        return tuple(acc)

    def both(i, carry):
        carry = step(own_ref, core * half, i, carry)
        return step(oth_ref, (1 - core) * half, i, carry)

    zero = jnp.zeros((SUB, LANE), jnp.float32)
    acc = lax.fori_loop(0, half // CHUNK, both, (zero,) * (CH + 3))
    carried = None
    for layer in (2, 1, 0):
        level = level_ref[layer]
        inverse = 1.0 / (1.0 + 2.0 * level)
        direct = -inverse * acc[CH + layer]
        if carried is None:
            carried = direct
        else:
            slope = (2.0 * TWO_PI) * inverse * lax.rsqrt(1.0 + 4.0 * level)
            carried = direct + slope * ((WEIGHT_VAR / 9) * box(carried))
    energy = (2.0 * WEIGHT_VAR / (9 * CH)) * box(carried)
    support = channels(sup_ref)
    for ch in range(CH):
        grad_ref[ch * SUB : (ch + 1) * SUB, :] = acc[ch] + energy * support[ch]


def local(support, coeffs, targets, labels):
    f32 = jnp.float32
    pixels = support.shape[2]
    side = math.isqrt(pixels)
    chips = lax.axis_size("tgt") * lax.axis_size("row")
    count = 2 * chips
    classes = pl.cdiv(labels.shape[1], LANE) * LANE
    row_of = {"theta": pl.cdiv(count, LANE) * LANE, "class": classes}
    width = row_of["theta"] + 2 * classes
    vmem = pl.BlockSpec(memory_space=pltpu.VMEM)
    limit = pltpu.CompilerParams(vmem_limit_bytes=16 * 2**20)

    image = targets.reshape(CH * SUB, LANE)
    own = lax.all_to_all(
        jnp.broadcast_to(image, (chips,) + image.shape), ("tgt", "row"), 0, 0, tiled=True
    )
    oth = lax.ppermute(own, "core", [(0, 1), (1, 0)])
    sup = support.reshape(CH * SUB, LANE)

    row, planes, levels = pl.pallas_call(
        functools.partial(pair_body, side, pixels, row_of),
        out_shape=(
            jax.ShapeDtypeStruct((1, width), f32),
            jax.ShapeDtypeStruct((count, 4, SUB, LANE), f32),
            jax.ShapeDtypeStruct((3, SUB, LANE), f32),
        ),
        in_specs=[vmem] * 5,
        out_specs=[vmem] * 3,
        scratch_shapes=[pltpu.VMEM((count, LANE), f32)],
        compiler_params=limit,
        name="pairs",
    )(own, oth, sup, coeffs, labels)

    rows = lax.all_to_all(
        jnp.broadcast_to(row[None], (count, 1, width)), ("core", "tgt", "row"), 0, 0, tiled=True
    )

    def index_of():
        tgt, rows_, core = (lax.axis_index(a) for a in ("tgt", "row", "core"))
        return (core * lax.axis_size("tgt") + tgt) * lax.axis_size("row") + rows_

    grad, residual = pl.pallas_call(
        functools.partial(final_body, side, row_of, index_of),
        out_shape=(
            jax.ShapeDtypeStruct(sup.shape, f32),
            jax.ShapeDtypeStruct(labels.shape, f32),
        ),
        in_specs=[vmem] * 6,
        out_specs=[vmem] * 2,
        scratch_shapes=[pltpu.VMEM((count, LANE), f32), pltpu.VMEM((count, classes), f32)],
        compiler_params=limit,
        name="final",
    )(rows, own, oth, sup, planes, levels)
    return grad.reshape(support.shape), residual


def solution(mesh):
    tgt, sup = mesh.devices.shape
    chips = Mesh(mesh.devices.reshape(tgt, sup // 2, 2), ("tgt", "row", "core"))
    by_support, by_target = ("row", "core", "tgt"), ("tgt", "row", "core")
    return jax.shard_map(
        local,
        mesh=chips,
        in_specs=(
            P(by_support, None, None),
            P(("row", "core"), None),
            P(by_target, None, None),
            P(by_target, None),
        ),
        out_specs=(P(by_support, None, None), P(by_target, None)),
        check_vma=False,
    )
```

```python
import functools
import math

import jax
import jax.numpy as jnp
from jax import lax
from jax.experimental import pallas as pl
from jax.experimental.pallas import tpu as pltpu
from jax.sharding import Mesh
from jax.sharding import PartitionSpec as P

WEIGHT_VAR = 1.6
BIAS_VAR = 0.1
DEPTH = 3
CH = 3
SUB = 8
LANE = 128
TWO_PI = 2.0 / math.pi
FIRST = WEIGHT_VAR / (9 * CH)
LATER = WEIGHT_VAR * TWO_PI / 9

NEAR = (1.6666752422e-1, 7.4953002686e-2, 4.5470025998e-2, 2.4181311049e-2, 4.2163199048e-2)
WIDE = (
    0.16666266322135925,
    0.07520359754562378,
    0.04114901274442673,
    0.058932434767484665,
    -0.10370756685733795,
    0.3290194272994995,
    -0.39874982833862305,
    0.2500518262386322,
)


def horner(z, coefficients):
    result = coefficients[-1]
    for value in coefficients[-2::-1]:
        result = result * z + value
    return result


def arcsine(x):
    a = jnp.abs(x)
    large, negative = a > 0.5, x < 0.0
    rest = jnp.maximum(2.0 - 2.0 * a, 1e-30)
    z = jnp.where(large, 0.25 * rest, x * x)
    root = rest * lax.rsqrt(rest)
    t = jnp.where(large, jnp.where(negative, root, -root), x)
    offset = jnp.where(large, jnp.where(negative, -0.5 * math.pi, 0.5 * math.pi), 0.0)
    return offset + (t + (t * z) * horner(z, NEAR))


def arcsine_inner(x):
    z = x * x
    return x + (x * z) * horner(z, WIDE)


class Grid:
    def __init__(self, side):
        lane = lax.broadcasted_iota(jnp.int32, (SUB, LANE), 1)
        sub = lax.broadcasted_iota(jnp.int32, (SUB, LANE), 0)
        self.side, self.fold = side, LANE // side
        column = lane % side
        self.place = lane // side
        self.not_left, self.not_right = column != 0, column != side - 1
        self.not_top, self.not_bottom = sub != 0, sub != SUB - 1

    def swap(self, arrays):
        arrays, step = list(arrays), 1
        while step < self.fold:
            low = (self.place // step) % 2 == 0
            shift = step * self.side
            for i in range(self.fold):
                if i & step == 0:
                    a, b = arrays[i], arrays[i + step]
                    axis = a.ndim - 1
                    arrays[i] = jnp.where(low, a, pltpu.roll(b, shift, axis))
                    arrays[i + step] = jnp.where(low, pltpu.roll(a, LANE - shift, axis), b)
            step *= 2
        return arrays

    def box(self, rows):
        h = []
        for x in rows:
            axis = x.ndim - 1
            h.append(
                x
                + jnp.where(self.not_left, pltpu.roll(x, 1, axis), 0.0)
                + jnp.where(self.not_right, pltpu.roll(x, LANE - 1, axis), 0.0)
            )
        axis = rows[0].ndim - 2
        above = jnp.where(self.not_top, pltpu.roll(h[-1], 1, axis), 0.0)
        below = jnp.where(self.not_bottom, pltpu.roll(h[0], SUB - 1, axis), 0.0)
        ring = [above] + h + [below]
        pairs = [ring[k] + ring[k + 1] for k in range(0, len(ring), 2)]
        out = []
        for q in range(self.fold):
            if q % 2 == 0:
                out.append(pairs[q // 2] + ring[q + 2])
            else:
                out.append(ring[q] + pairs[(q + 1) // 2])
        return out


def affine(factor, rows):
    return [factor * x + BIAS_VAR for x in rows]


def self_levels(grid, image):
    energy = [sum(x * x for x in rows) for rows in zip(*image)]
    level = affine(FIRST, grid.box(energy))
    levels, gains = [], []
    for layer in range(DEPTH):
        gain = [lax.rsqrt(1.0 + 2.0 * x) for x in level]
        levels.append(level)
        gains.append(gain)
        if layer + 1 < DEPTH:
            inner = [(2.0 * x) * (g * g) for x, g in zip(level, gain)]
            angle = [(arcsine if layer == 0 else arcsine_inner)(x) for x in inner]
            level = affine(LATER, grid.box(angle))
    return levels, gains


def pairs_of(grid, pixels, block, image_ref, state, plane_ref, sum_of):
    support, gains2, decay, slope_of = state
    fold = grid.fold

    def step(k, carry):
        at = pl.ds(k * block, block)
        to = pl.ds(k * (block // fold), block // fold)
        target = []
        for c in range(CH):
            x = image_ref[at, c * SUB : (c + 1) * SUB, :].reshape(block // fold, fold, SUB, LANE)
            target.append(grid.swap([x[:, i] for i in range(fold)]))
        _, tgt_gains = self_levels(grid, target)
        level = [
            sum(s * t for s, t in zip(row_s, row_t))
            for row_s, row_t in zip(zip(*support), zip(*target))
        ]
        level = affine(FIRST, grid.box(level))
        gains, corrs = [], []
        for layer in range(DEPTH):
            gain = [s * t for s, t in zip(gains2[layer], tgt_gains[layer])]
            corr = [x * g for x, g in zip(level, gain)]
            gains.append(gain)
            corrs.append(corr)
            angle = [(arcsine if layer == 0 else arcsine_inner)(x) for x in corr]
            if layer + 1 < DEPTH:
                level = affine(LATER, grid.box(angle))
        sum_of(k, jnp.sum(sum(angle), axis=1))
        grad = [WEIGHT_VAR * TWO_PI / pixels] * fold
        carried = None
        for layer in range(DEPTH - 1, -1, -1):
            slope = [
                g * lax.rsqrt((1.0 - x) * (1.0 + x)) for g, x in zip(grad, corrs[layer])
            ]
            direct = [d * (s * x) for d, s, x in zip(decay[layer], slope, corrs[layer])]
            if carried is None:
                carried = direct
            else:
                back = grid.box(carried)
                carried = [d + m * x for d, m, x in zip(direct, slope_of[layer], back)]
            factor = LATER if layer > 0 else FIRST
            grad = [
                factor * x for x in grid.box([s * g for s, g in zip(slope, gains[layer])])
            ]
        energy = [(2.0 * FIRST) * x for x in grid.box(carried)]
        for c in range(CH):
            for q in range(fold):
                plane_ref[to, c, q] = grad[q] * target[c][q] + energy[q] * support[c][q]
        return carry

    lax.fori_loop(0, image_ref.shape[0] // block, step, 0)


def first_body(
    classes, tgt_hbm, sup_hbm, coef_hbm, lab_hbm,
    image_ref, sup_ref, head_ref, tgt_ref, coef_ref, lab_ref, sems,
):
    pairs = ((tgt_hbm, tgt_ref), (sup_hbm, sup_ref), (coef_hbm, coef_ref), (lab_hbm, lab_ref))
    copies = [pltpu.make_async_copy(a, b, sems.at[k]) for k, (a, b) in enumerate(pairs)]
    for copy in copies:
        copy.start()
    head_ref[...] = jnp.zeros_like(head_ref)
    copies[0].wait()
    image = tgt_ref[...]
    for k in range(image_ref.shape[0]):
        image_ref[k] = image
    for copy in copies[1:]:
        copy.wait()
    labels = lab_ref.shape[-1]
    head_ref[0:1, 0:labels] = coef_ref[pl.ds(lax.axis_index("tgt"), 1), :]
    head_ref[0:1, classes : classes + labels] = lab_ref[...]


def own_body(side, pixels, block, own_ref, sup_ref, sum_ref, plane_ref, state_ref):
    grid = Grid(side)
    support = [
        grid.swap([sup_ref[c * SUB : (c + 1) * SUB, :]] * grid.fold) for c in range(CH)
    ]
    levels, gains = self_levels(grid, support)
    gains2, decay, slope_of = [], [], []
    for level, gain in zip(levels, gains):
        gains2.append([2.0 * g for g in gain])
        decay.append([-(g * g) for g in gain])
        slope_of.append(
            [(2.0 * LATER) * (g * g) * lax.rsqrt(1.0 + 4.0 * x) for x, g in zip(level, gain)]
        )
    state = (support, gains2, decay, slope_of)
    for part, arrays in enumerate(state):
        for layer in range(DEPTH):
            for q in range(grid.fold):
                state_ref[part, layer, q] = arrays[layer][q]

    def sum_of(k, rows):
        for g in range(rows.shape[0]):
            sum_ref[pl.ds(k * rows.shape[0] + g, 1)] = rows[g : g + 1]

    pairs_of(grid, pixels, block, own_ref, state, plane_ref, sum_of)


def other_body(
    side, pixels, block, width, oth_ref, state_ref, own_sum_ref, head_ref,
    row_ref, plane_ref, sums,
):
    grid = Grid(side)
    half = oth_ref.shape[0]
    groups = half // grid.fold
    core = lax.axis_index("core")
    for g in range(groups):
        sums[pl.ds(core * groups + g, 1)] = own_sum_ref[g : g + 1]
    state = [
        [[state_ref[part, layer, q] for q in range(grid.fold)] for layer in range(DEPTH)]
        for part in range(4)
    ]

    def sum_of(k, rows):
        base = (1 - core) * groups + k * rows.shape[0]
        for g in range(rows.shape[0]):
            sums[pl.ds(base + g, 1)] = rows[g : g + 1]

    pairs_of(grid, pixels, block, oth_ref, state, plane_ref, sum_of)

    count = 2 * half
    lane = lax.broadcasted_iota(jnp.int32, (LANE, count), 0)
    image = lax.broadcasted_iota(jnp.int32, (LANE, count), 1)
    select = jnp.where(lane // side == image % grid.fold, 1.0, 0.0)
    total = lax.dot_general(
        sums[...],
        select,
        (((1,), (0,)), ((), ())),
        precision=lax.Precision.HIGHEST,
        preferred_element_type=jnp.float32,
    )
    group = lax.broadcasted_iota(jnp.int32, total.shape, 0)
    image = lax.broadcasted_iota(jnp.int32, total.shape, 1)
    total = jnp.sum(
        jnp.where(image // grid.fold == group, total, 0.0), axis=0, keepdims=True
    )
    row_ref[:, 0:width] = jnp.zeros((1, width), jnp.float32)
    row_ref[:, 0:count] = (WEIGHT_VAR * TWO_PI / pixels) * total + BIAS_VAR
    row_ref[:, width:] = head_ref[...]


def final_body(
    side, row_of, index_of, all_ref, plane0_ref, plane1_ref, grad_ref, res_ref,
    weight, group_weight, misfits,
):
    grid = Grid(side)
    fold = grid.fold
    groups = plane0_ref.shape[0]
    count = 2 * groups * fold
    core = lax.axis_index("core")
    me = index_of()
    width, classes = row_of["theta"], row_of["class"]
    theta = all_ref[:, 0, 0:count]
    coeffs = all_ref[:, 0, width : width + classes]
    labels = all_ref[:, 0, width + classes : width + 2 * classes]
    misfit = (
        lax.dot_general(
            theta,
            coeffs,
            (((0,), (0,)), ((), ())),
            precision=lax.Precision.HIGHEST,
            preferred_element_type=jnp.float32,
        )
        - labels
    )
    own_coeffs = all_ref[me, :, width : width + classes]
    cot = jnp.sum(misfit * own_coeffs, axis=1, keepdims=True)
    weight[...] = jnp.broadcast_to(cot, weight.shape)
    place = lax.broadcasted_iota(jnp.int32, group_weight.shape, 1) // side
    rows = weight[pl.ds(0, 2 * groups, stride=fold), :]
    for i in range(1, fold):
        rows = jnp.where(place == i, weight[pl.ds(i, 2 * groups, stride=fold), :], rows)
    group_weight[...] = rows
    misfits[...] = misfit
    res_ref[...] = misfits[pl.ds(me, 1), 0 : res_ref.shape[-1]]

    block = math.gcd(groups, 4)

    def step(plane_ref, base, k, acc):
        acc = list(acc)
        for g in range(block):
            c = group_weight[pl.ds(base + k * block + g, SUB, stride=0), :]
            for n in range(CH * fold):
                acc[n] = acc[n] + c * plane_ref[k * block + g, n // fold, n % fold]
        return acc

    def both(k, acc):
        acc = step(plane0_ref, core * groups, k, acc)
        return tuple(step(plane1_ref, (1 - core) * groups, k, acc))

    zero = jnp.zeros((SUB, LANE), jnp.float32)
    acc = lax.fori_loop(0, groups // block, both, (zero,) * (CH * fold))
    for c in range(CH):
        out = None
        for q in range(fold):
            x, shift = acc[c * fold + q], LANE // 2
            while shift >= side:
                x = x + pltpu.roll(x, shift, 1)
                shift //= 2
            out = x if out is None else jnp.where(grid.place == q, x, out)
        grad_ref[c * SUB : (c + 1) * SUB, :] = out


def local(support, coeffs, targets, labels):
    f32 = jnp.float32
    pixels = support.shape[2]
    side = math.isqrt(pixels)
    fold = LANE // side
    chips = lax.axis_size("tgt") * lax.axis_size("row")
    count = 2 * chips
    classes = pl.cdiv(labels.shape[1], LANE) * LANE
    row_of = {"theta": pl.cdiv(count, LANE) * LANE, "class": classes}
    width = row_of["theta"] + 2 * classes
    block = math.gcd(chips, 4 * fold)
    groups = chips // fold
    assert support.shape[0] == 1 and targets.shape[0] == 1
    assert side * side == pixels == SUB * LANE and groups * fold == chips

    vmem = pl.BlockSpec(memory_space=pltpu.VMEM)
    hbm = pl.BlockSpec(memory_space=pltpu.HBM)
    limit = pltpu.CompilerParams(vmem_limit_bytes=16 * 2**20)
    effort = pl.CostEstimate(
        flops=300 * chips * pixels, bytes_accessed=24 * chips * pixels, transcendentals=0
    )

    sup_shape = (CH * SUB, LANE)
    inputs = (targets.reshape(sup_shape), support.reshape(sup_shape), coeffs, labels)
    images, sup, head = pl.pallas_call(
        functools.partial(first_body, classes),
        out_shape=(
            jax.ShapeDtypeStruct((chips,) + sup_shape, f32),
            jax.ShapeDtypeStruct(sup_shape, f32),
            jax.ShapeDtypeStruct((1, 2 * classes), f32),
        ),
        in_specs=[hbm] * 4,
        out_specs=[vmem] * 3,
        scratch_shapes=[
            pltpu.VMEM(sup_shape, f32),
            pltpu.VMEM(coeffs.shape, f32),
            pltpu.VMEM(labels.shape, f32),
            pltpu.SemaphoreType.DMA((4,)),
        ],
        compiler_params=limit,
        name="first",
    )(*(pltpu.with_memory_space_constraint(x, pltpu.HBM) for x in inputs))
    own = lax.all_to_all(images, ("tgt", "row"), 0, 0, tiled=True)
    oth = lax.ppermute(own, "core", [(0, 1), (1, 0)])

    planes = jax.ShapeDtypeStruct((groups, CH, fold, SUB, LANE), f32)
    sums, planes0, state = pl.pallas_call(
        functools.partial(own_body, side, pixels, block),
        out_shape=(
            jax.ShapeDtypeStruct((groups, LANE), f32),
            planes,
            jax.ShapeDtypeStruct((4, DEPTH, fold, SUB, LANE), f32),
        ),
        in_specs=[vmem] * 2,
        out_specs=[vmem] * 3,
        compiler_params=limit,
        cost_estimate=effort,
        name="own",
    )(own, sup)
    row, planes1 = pl.pallas_call(
        functools.partial(other_body, side, pixels, block, row_of["theta"]),
        out_shape=(jax.ShapeDtypeStruct((1, width), f32), planes),
        in_specs=[vmem] * 4,
        out_specs=[vmem] * 2,
        scratch_shapes=[pltpu.VMEM((2 * groups, LANE), f32)],
        compiler_params=limit,
        cost_estimate=effort,
        name="other",
    )(oth, state, sums, head)

    rows = lax.all_to_all(
        jnp.broadcast_to(row[None], (count, 1, width)), ("core", "tgt", "row"), 0, 0, tiled=True
    )

    def index_of():
        tgt, place, core = (lax.axis_index(a) for a in ("tgt", "row", "core"))
        return (core * lax.axis_size("tgt") + tgt) * lax.axis_size("row") + place

    grad, residual = pl.pallas_call(
        functools.partial(final_body, side, row_of, index_of),
        out_shape=(
            jax.ShapeDtypeStruct(sup.shape, f32),
            jax.ShapeDtypeStruct(labels.shape, f32),
        ),
        in_specs=[vmem] * 3,
        out_specs=[vmem] * 2,
        scratch_shapes=[
            pltpu.VMEM((count, LANE), f32),
            pltpu.VMEM((2 * groups, LANE), f32),
            pltpu.VMEM((count, classes), f32),
        ],
        compiler_params=limit,
        name="final",
    )(rows, planes0, planes1)
    return grad.reshape(support.shape), residual


def solution(mesh):
    tgt, sup = mesh.devices.shape
    chips = Mesh(mesh.devices.reshape(tgt, sup // 2, 2), ("tgt", "row", "core"))
    by_support, by_target = ("row", "core", "tgt"), ("tgt", "row", "core")
    return jax.shard_map(
        local,
        mesh=chips,
        in_specs=(
            P(by_support, None, None),
            P(("row", "core"), None),
            P(by_target, None, None),
            P(by_target, None),
        ),
        out_specs=(P(by_support, None, None), P(by_target, None)),
        check_vma=False,
    )
```

```python
import functools
import math

import jax
import jax.numpy as jnp
from jax import lax
from jax.experimental import pallas as pl
from jax.experimental.pallas import tpu as pltpu
from jax.sharding import Mesh
from jax.sharding import PartitionSpec as P

WEIGHT_VAR = 1.6
BIAS_VAR = 0.1
DEPTH = 3
CH = 3
SUB = 8
LANE = 128
TWO_PI = 2.0 / math.pi
PARTS = 5
FIRST = WEIGHT_VAR / (9 * CH)
LATER = WEIGHT_VAR * TWO_PI / 9

NEAR = (1.6666752422e-1, 7.4953002686e-2, 4.5470025998e-2, 2.4181311049e-2, 4.2163199048e-2)
WIDE = (
    1.0,
    0.16666266322135925,
    0.07520359754562378,
    0.04114901274442673,
    0.058932434767484665,
    -0.10370756685733795,
    0.3290194272994995,
    -0.39874982833862305,
    0.2500518262386322,
)
HALF = (
    1.0000000202678234,
    0.1666621810142767,
    0.07516158417922122,
    0.042482407794996346,
    0.04384003568012658,
    -0.018689176226557736,
    0.07216594689625302,
)


def horner(z, coefficients, scale=1.0):
    result = scale * coefficients[-1]
    for value in coefficients[-2::-1]:
        result = result * z + scale * value
    return result


def arcsine(x):
    a = jnp.abs(x)
    large, negative = a > 0.5, x < 0.0
    left = 1.0 - a
    z = jnp.where(large, 0.5 * left, x * x)
    root = (2.0 * left) * lax.rsqrt(2.0 * left)
    t = jnp.where(large, jnp.where(negative, root, -root), x)
    right = LATER * 0.5 * math.pi
    offset = jnp.where(large, jnp.where(negative, -right, right), 0.0)
    return offset + t * (LATER + z * horner(z, NEAR, LATER)), left * (1.0 + a)


def arcsine_inner(x, scale):
    z = x * x
    return x * horner(z, WIDE, scale), 1.0 - z


class Grid:
    def __init__(self, side):
        lane = lax.broadcasted_iota(jnp.int32, (SUB, LANE), 1)
        sub = lax.broadcasted_iota(jnp.int32, (SUB, LANE), 0)
        self.side, self.fold = side, LANE // side
        column = lane % side
        self.place = lane // side
        self.not_left, self.not_right = column != 0, column != side - 1
        self.not_top, self.not_bottom = sub != 0, sub != SUB - 1

    def neighbours(self):
        across = jnp.where(self.not_left, 1.0, 0.0) + jnp.where(self.not_right, 2.0, 1.0)
        rows = [across * 3.0] * self.fold
        rows[0] = across * jnp.where(self.not_top, 3.0, 2.0)
        rows[-1] = across * jnp.where(self.not_bottom, 3.0, 2.0)
        return rows

    def swap(self, arrays):
        arrays, step = list(arrays), 1
        while step < self.fold:
            low = (self.place // step) % 2 == 0
            shift = step * self.side
            for i in range(self.fold):
                if i & step == 0:
                    a, b = arrays[i], arrays[i + step]
                    axis = a.ndim - 1
                    arrays[i] = jnp.where(low, a, pltpu.roll(b, shift, axis))
                    arrays[i + step] = jnp.where(low, pltpu.roll(a, LANE - shift, axis), b)
            step *= 2
        return arrays

    def box(self, rows):
        h = []
        for x in rows:
            axis = x.ndim - 1
            h.append(
                x
                + jnp.where(self.not_left, pltpu.roll(x, 1, axis), 0.0)
                + jnp.where(self.not_right, pltpu.roll(x, LANE - 1, axis), 0.0)
            )
        axis = rows[0].ndim - 2
        above = jnp.where(self.not_top, pltpu.roll(h[-1], 1, axis), 0.0)
        below = jnp.where(self.not_bottom, pltpu.roll(h[0], SUB - 1, axis), 0.0)
        ring = [above] + h + [below]
        pairs = [ring[k] + ring[k + 1] for k in range(0, len(ring), 2)]
        out = []
        for q in range(self.fold):
            if q % 2 == 0:
                out.append(pairs[q // 2] + ring[q + 2])
            else:
                out.append(ring[q] + pairs[(q + 1) // 2])
        return out


def self_gains(grid, image):
    energy = [sum(x * x for x in rows) for rows in zip(*image)]
    start = 1.0 + 2.0 * BIAS_VAR
    gain = [lax.rsqrt((2.0 * FIRST) * x + start) for x in grid.box(energy)]
    gains = [gain]
    most = [(LATER * math.pi) * n + start for n in grid.neighbours()]
    powers = [c * 0.5**k for k, c in enumerate(HALF)]
    for _ in range(DEPTH - 1):
        less = [g * horner(g * g, powers, 4.0 * LATER * math.sqrt(0.5)) for g in gain]
        gain = [lax.rsqrt(m - x) for m, x in zip(most, grid.box(less))]
        gains.append(gain)
    return gains


def pairs_of(grid, block, image_ref, state, plane_ref, sum_of):
    scaled, double, gains2, decay, slope_of = state
    fold = grid.fold

    def step(k, carry):
        at = pl.ds(k * block, block)
        to = pl.ds(k * (block // fold), block // fold)
        target = []
        for c in range(CH):
            x = image_ref[at, c * SUB : (c + 1) * SUB, :].reshape(block // fold, fold, SUB, LANE)
            target.append(grid.swap([x[:, i] for i in range(fold)]))
        tgt_gains = self_gains(grid, target)
        spread = grid.box(
            [
                sum(s * t for s, t in zip(row_s, row_t))
                for row_s, row_t in zip(zip(*scaled), zip(*target))
            ]
        )
        gains, corrs, rests = [], [], []
        for layer in range(DEPTH):
            gain = [s * t for s, t in zip(gains2[layer], tgt_gains[layer])]
            corr = [(x + BIAS_VAR) * g for x, g in zip(spread, gain)]
            if layer == 0:
                both = [arcsine(x) for x in corr]
            else:
                scale = LATER if layer + 1 < DEPTH else 1.0
                both = [arcsine_inner(x, scale) for x in corr]
            angle = [x for x, _ in both]
            gains.append(gain)
            corrs.append(corr)
            rests.append([x for _, x in both])
            if layer + 1 < DEPTH:
                spread = grid.box(angle)
        sum_of(k, jnp.sum(sum(angle), axis=1))
        slope = [lax.rsqrt(x) for x in rests[-1]]
        carried = [d * (s * x) for d, s, x in zip(decay[-1], slope, corrs[-1])]
        for layer in range(DEPTH - 2, -1, -1):
            grad = grid.box([s * g for s, g in zip(slope, gains[layer + 1])])
            slope = [g * lax.rsqrt(x) for g, x in zip(grad, rests[layer])]
            carried = [
                d * (s * x) + m * y
                for d, s, x, m, y in zip(
                    decay[layer], slope, corrs[layer], slope_of[layer], grid.box(carried)
                )
            ]
        grad = grid.box([s * g for s, g in zip(slope, gains[0])])
        energy = grid.box(carried)
        for c in range(CH):
            for q in range(fold):
                plane_ref[to, c, q] = grad[q] * target[c][q] + energy[q] * double[c][q]
        return carry

    lax.fori_loop(0, image_ref.shape[0] // block, step, 0)


def first_body(
    classes, tgt_hbm, sup_hbm, coef_hbm, lab_hbm,
    image_ref, sup_ref, head_ref, tgt_ref, coef_ref, lab_ref, sems,
):
    pairs = ((tgt_hbm, tgt_ref), (sup_hbm, sup_ref), (coef_hbm, coef_ref), (lab_hbm, lab_ref))
    copies = [pltpu.make_async_copy(a, b, sems.at[k]) for k, (a, b) in enumerate(pairs)]
    for copy in copies:
        copy.start()
    head_ref[...] = jnp.zeros_like(head_ref)
    copies[0].wait()
    image = tgt_ref[...]
    for k in range(image_ref.shape[0]):
        image_ref[k] = image
    for copy in copies[1:]:
        copy.wait()
    labels = lab_ref.shape[-1]
    head_ref[0:1, 0:labels] = coef_ref[pl.ds(lax.axis_index("tgt"), 1), :]
    head_ref[0:1, classes : classes + labels] = lab_ref[...]


def own_body(side, block, own_ref, sup_ref, sum_ref, plane_ref, state_ref):
    grid = Grid(side)
    support = [
        grid.swap([sup_ref[c * SUB : (c + 1) * SUB, :]] * grid.fold) for c in range(CH)
    ]
    gains = self_gains(grid, support)
    state = (
        [[FIRST * x for x in rows] for rows in support],
        [[2.0 * x for x in rows] for rows in support],
        [[2.0 * g for g in gain] for gain in gains],
        [[-(g * g) for g in gain] for gain in gains],
        [[2.0 * (g * g * g) * lax.rsqrt(2.0 - g * g) for g in gain] for gain in gains],
    )
    for part, arrays in enumerate(state):
        for k in range(DEPTH):
            for q in range(grid.fold):
                state_ref[part, k, q] = arrays[k][q]

    def sum_of(k, rows):
        for g in range(rows.shape[0]):
            sum_ref[pl.ds(k * rows.shape[0] + g, 1)] = rows[g : g + 1]

    pairs_of(grid, block, own_ref, state, plane_ref, sum_of)


def other_body(
    side, pixels, block, width, oth_ref, state_ref, own_sum_ref, head_ref,
    row_ref, plane_ref, sums,
):
    grid = Grid(side)
    half = oth_ref.shape[0]
    groups = half // grid.fold
    core = lax.axis_index("core")
    for g in range(groups):
        sums[pl.ds(core * groups + g, 1)] = own_sum_ref[g : g + 1]
    state = [
        [[state_ref[part, layer, q] for q in range(grid.fold)] for layer in range(DEPTH)]
        for part in range(PARTS)
    ]

    def sum_of(k, rows):
        base = (1 - core) * groups + k * rows.shape[0]
        for g in range(rows.shape[0]):
            sums[pl.ds(base + g, 1)] = rows[g : g + 1]

    pairs_of(grid, block, oth_ref, state, plane_ref, sum_of)

    count = 2 * half
    lane = lax.broadcasted_iota(jnp.int32, (LANE, count), 0)
    image = lax.broadcasted_iota(jnp.int32, (LANE, count), 1)
    select = jnp.where(lane // side == image % grid.fold, 1.0, 0.0)
    total = lax.dot_general(
        sums[...],
        select,
        (((1,), (0,)), ((), ())),
        precision=lax.Precision.HIGHEST,
        preferred_element_type=jnp.float32,
    )
    group = lax.broadcasted_iota(jnp.int32, total.shape, 0)
    image = lax.broadcasted_iota(jnp.int32, total.shape, 1)
    total = jnp.sum(
        jnp.where(image // grid.fold == group, total, 0.0), axis=0, keepdims=True
    )
    row_ref[:, 0:width] = jnp.zeros((1, width), jnp.float32)
    row_ref[:, 0:count] = (WEIGHT_VAR * TWO_PI / pixels) * total + BIAS_VAR
    row_ref[:, width:] = head_ref[...]


def final_body(
    side, pixels, row_of, index_of, all_ref, plane0_ref, plane1_ref, grad_ref, res_ref,
    group_weight,
):
    grid = Grid(side)
    fold = grid.fold
    groups = plane0_ref.shape[0]
    count = 2 * groups * fold
    core = lax.axis_index("core")
    me = index_of()
    width, classes = row_of["theta"], row_of["class"]
    theta = all_ref[:, 0, 0:count]
    coeffs = all_ref[:, 0, width : width + classes]
    labels = all_ref[:, 0, width + classes : width + 2 * classes]
    own_coeffs = all_ref[me, :, width : width + classes]
    gram = jnp.sum(coeffs * own_coeffs, axis=1, keepdims=True)
    known = jnp.sum(labels * own_coeffs, axis=1, keepdims=True)
    source = lax.broadcasted_iota(jnp.int32, theta.shape, 0)
    image = lax.broadcasted_iota(jnp.int32, theta.shape, 1)
    terms = theta * gram - jnp.where(source == image, known, 0.0)
    cot = jnp.broadcast_to(jnp.sum(terms, axis=0, keepdims=True), (SUB, count))
    if count % LANE:
        cot = jnp.concatenate([cot, jnp.zeros((SUB, LANE - count % LANE), jnp.float32)], axis=1)
    for g in range(2 * groups):
        tile, lane = divmod(g * fold, LANE)
        part = cot[:, tile * LANE : (tile + 1) * LANE]
        group_weight[g : g + 1] = jnp.take_along_axis(part, grid.place + lane, axis=1)[0:1]

    share = jnp.sum(jnp.where(image == me, theta, 0.0), axis=1, keepdims=True)
    predicted = jnp.sum(share * coeffs, axis=0, keepdims=True)
    own_labels = all_ref[me, :, width + classes : width + 2 * classes]
    res_ref[...] = (predicted - own_labels)[:, 0 : res_ref.shape[-1]]

    block = math.gcd(groups, 4)

    def step(plane_ref, base, k, acc):
        acc = list(acc)
        for g in range(block):
            c = group_weight[pl.ds(base + k * block + g, SUB, stride=0), :]
            for n in range(CH * fold):
                acc[n] = acc[n] + c * plane_ref[k * block + g, n // fold, n % fold]
        return acc

    def both(k, acc):
        acc = step(plane0_ref, core * groups, k, acc)
        return tuple(step(plane1_ref, (1 - core) * groups, k, acc))

    factor = (WEIGHT_VAR * TWO_PI / pixels) * LATER ** (DEPTH - 1) * FIRST
    zero = jnp.zeros((SUB, LANE), jnp.float32)
    acc = lax.fori_loop(0, groups // block, both, (zero,) * (CH * fold))
    for c in range(CH):
        out = None
        for q in range(fold):
            x, shift = acc[c * fold + q], LANE // 2
            while shift >= side:
                x = x + pltpu.roll(x, shift, 1)
                shift //= 2
            out = x if out is None else jnp.where(grid.place == q, x, out)
        grad_ref[c * SUB : (c + 1) * SUB, :] = factor * out


def local(support, coeffs, targets, labels):
    f32 = jnp.float32
    pixels = support.shape[2]
    side = math.isqrt(pixels)
    fold = LANE // side
    chips = lax.axis_size("tgt") * lax.axis_size("row")
    count = 2 * chips
    classes = pl.cdiv(labels.shape[1], LANE) * LANE
    row_of = {"theta": pl.cdiv(count, LANE) * LANE, "class": classes}
    width = row_of["theta"] + 2 * classes
    block = math.gcd(chips, 4 * fold)
    groups = chips // fold
    assert support.shape[0] == 1 and targets.shape[0] == 1
    assert side * side == pixels == SUB * LANE and groups * fold == chips

    vmem = pl.BlockSpec(memory_space=pltpu.VMEM)
    hbm = pl.BlockSpec(memory_space=pltpu.HBM)
    limit = pltpu.CompilerParams(vmem_limit_bytes=16 * 2**20)
    effort = pl.CostEstimate(
        flops=300 * chips * pixels, bytes_accessed=24 * chips * pixels, transcendentals=0
    )

    sup_shape = (CH * SUB, LANE)
    inputs = (targets.reshape(sup_shape), support.reshape(sup_shape), coeffs, labels)
    images, sup, head = pl.pallas_call(
        functools.partial(first_body, classes),
        out_shape=(
            jax.ShapeDtypeStruct((chips,) + sup_shape, f32),
            jax.ShapeDtypeStruct(sup_shape, f32),
            jax.ShapeDtypeStruct((1, 2 * classes), f32),
        ),
        in_specs=[hbm] * 4,
        out_specs=[vmem] * 3,
        scratch_shapes=[
            pltpu.VMEM(sup_shape, f32),
            pltpu.VMEM(coeffs.shape, f32),
            pltpu.VMEM(labels.shape, f32),
            pltpu.SemaphoreType.DMA((4,)),
        ],
        compiler_params=limit,
        name="first",
    )(*(pltpu.with_memory_space_constraint(x, pltpu.HBM) for x in inputs))
    own = lax.all_to_all(images, ("tgt", "row"), 0, 0, tiled=True)
    oth = lax.ppermute(own, "core", [(0, 1), (1, 0)])

    planes = jax.ShapeDtypeStruct((groups, CH, fold, SUB, LANE), f32)
    sums, planes0, state = pl.pallas_call(
        functools.partial(own_body, side, block),
        out_shape=(
            jax.ShapeDtypeStruct((groups, LANE), f32),
            planes,
            jax.ShapeDtypeStruct((PARTS, DEPTH, fold, SUB, LANE), f32),
        ),
        in_specs=[vmem] * 2,
        out_specs=[vmem] * 3,
        compiler_params=limit,
        cost_estimate=effort,
        name="own",
    )(own, sup)
    row, planes1 = pl.pallas_call(
        functools.partial(other_body, side, pixels, block, row_of["theta"]),
        out_shape=(jax.ShapeDtypeStruct((1, width), f32), planes),
        in_specs=[vmem] * 4,
        out_specs=[vmem] * 2,
        scratch_shapes=[pltpu.VMEM((2 * groups, LANE), f32)],
        compiler_params=limit,
        cost_estimate=effort,
        name="other",
    )(oth, state, sums, head)

    rows = lax.all_to_all(
        jnp.broadcast_to(row[None], (count, 1, width)), ("core", "tgt", "row"), 0, 0, tiled=True
    )

    def index_of():
        tgt, place, core = (lax.axis_index(a) for a in ("tgt", "row", "core"))
        return (core * lax.axis_size("tgt") + tgt) * lax.axis_size("row") + place

    grad, residual = pl.pallas_call(
        functools.partial(final_body, side, pixels, row_of, index_of),
        out_shape=(
            jax.ShapeDtypeStruct(sup.shape, f32),
            jax.ShapeDtypeStruct(labels.shape, f32),
        ),
        in_specs=[vmem] * 3,
        out_specs=[vmem] * 2,
        scratch_shapes=[pltpu.VMEM((2 * groups, LANE), f32)],
        compiler_params=limit,
        name="final",
    )(rows, planes0, planes1)
    return grad.reshape(support.shape), residual


def solution(mesh):
    tgt, sup = mesh.devices.shape
    chips = Mesh(mesh.devices.reshape(tgt, sup // 2, 2), ("tgt", "row", "core"))
    by_support, by_target = ("row", "core", "tgt"), ("tgt", "row", "core")
    return jax.shard_map(
        local,
        mesh=chips,
        in_specs=(
            P(by_support, None, None),
            P(("row", "core"), None),
            P(by_target, None, None),
            P(by_target, None),
        ),
        out_specs=(P(by_support, None, None), P(by_target, None)),
        check_vma=False,
    )
```

```python
import functools
import math

import jax
import jax.numpy as jnp
from jax import lax
from jax.experimental import pallas as pl
from jax.experimental.pallas import tpu as pltpu
from jax.sharding import Mesh
from jax.sharding import PartitionSpec as P

WEIGHT_VAR = 1.6
BIAS_VAR = 0.1
DEPTH = 3
CH = 3
SUB = 8
LANE = 128
TWO_PI = 2.0 / math.pi
PARTS = 4
FIRST = WEIGHT_VAR / (9 * CH)
LATER = WEIGHT_VAR * TWO_PI / 9

NEAR = (1.6666752422e-1, 7.4953002686e-2, 4.5470025998e-2, 2.4181311049e-2, 4.2163199048e-2)
WIDE = (
    1.0,
    0.16666266322135925,
    0.07520359754562378,
    0.04114901274442673,
    0.058932434767484665,
    -0.10370756685733795,
    0.3290194272994995,
    -0.39874982833862305,
    0.2500518262386322,
)
HALF = (
    1.0000000202678234,
    0.1666621810142767,
    0.07516158417922122,
    0.042482407794996346,
    0.04384003568012658,
    -0.018689176226557736,
    0.07216594689625302,
)


def horner(z, coefficients, scale=1.0):
    result = scale * coefficients[-1]
    for value in coefficients[-2::-1]:
        result = result * z + scale * value
    return result


def arcsine(x):
    a = jnp.abs(x)
    large, negative = a > 0.5, x < 0.0
    left = 1.0 - a
    z = jnp.where(large, 0.5 * left, x * x)
    root = (2.0 * left) * lax.rsqrt(2.0 * left)
    t = jnp.where(large, jnp.where(negative, root, -root), x)
    right = LATER * 0.5 * math.pi
    offset = jnp.where(large, jnp.where(negative, -right, right), 0.0)
    return offset + t * (LATER + z * horner(z, NEAR, LATER)), left * (1.0 + a)


def arcsine_inner(x, scale):
    z = x * x
    return x * horner(z, WIDE, scale), 1.0 - z


class Grid:
    def __init__(self, side):
        lane = lax.broadcasted_iota(jnp.int32, (SUB, LANE), 1)
        sub = lax.broadcasted_iota(jnp.int32, (SUB, LANE), 0)
        self.side, self.fold = side, LANE // side
        column = lane % side
        self.place = lane // side
        self.not_left, self.not_right = column != 0, column != side - 1
        self.not_top, self.not_bottom = sub != 0, sub != SUB - 1

    def neighbours(self):
        across = jnp.where(self.not_left, 1.0, 0.0) + jnp.where(self.not_right, 2.0, 1.0)
        rows = [across * 3.0] * self.fold
        rows[0] = across * jnp.where(self.not_top, 3.0, 2.0)
        rows[-1] = across * jnp.where(self.not_bottom, 3.0, 2.0)
        return rows

    def swap(self, arrays):
        arrays, step = list(arrays), 1
        while step < self.fold:
            low = (self.place // step) % 2 == 0
            shift = step * self.side
            for i in range(self.fold):
                if i & step == 0:
                    a, b = arrays[i], arrays[i + step]
                    axis = a.ndim - 1
                    arrays[i] = jnp.where(low, a, pltpu.roll(b, shift, axis))
                    arrays[i + step] = jnp.where(low, pltpu.roll(a, LANE - shift, axis), b)
            step *= 2
        return arrays

    def box(self, rows):
        h = []
        for x in rows:
            axis = x.ndim - 1
            h.append(
                x
                + jnp.where(self.not_left, pltpu.roll(x, 1, axis), 0.0)
                + jnp.where(self.not_right, pltpu.roll(x, LANE - 1, axis), 0.0)
            )
        axis = rows[0].ndim - 2
        above = jnp.where(self.not_top, pltpu.roll(h[-1], 1, axis), 0.0)
        below = jnp.where(self.not_bottom, pltpu.roll(h[0], SUB - 1, axis), 0.0)
        ring = [above] + h + [below]
        pairs = [ring[k] + ring[k + 1] for k in range(0, len(ring), 2)]
        out = []
        for q in range(self.fold):
            if q % 2 == 0:
                out.append(pairs[q // 2] + ring[q + 2])
            else:
                out.append(ring[q] + pairs[(q + 1) // 2])
        return out


def self_gains(grid, energy):
    start = 1.0 + 2.0 * BIAS_VAR
    gain = [lax.rsqrt((2.0 * FIRST) * x + start) for x in grid.box(energy)]
    gains = [gain]
    most = [(LATER * math.pi) * n + start for n in grid.neighbours()]
    powers = [c * 0.5**k for k, c in enumerate(HALF)]
    for _ in range(DEPTH - 1):
        less = [g * horner(g * g, powers, 4.0 * LATER * math.sqrt(0.5)) for g in gain]
        gain = [lax.rsqrt(m - x) for m, x in zip(most, grid.box(less))]
        gains.append(gain)
    return gains


def pairs_of(grid, block, image_ref, state, plane_ref, sum_of):
    scaled, double, gains2, decay, slope_of = state
    fold = grid.fold

    def step(k, carry):
        at = pl.ds(k * block, block)
        to = pl.ds(k * (block // fold), block // fold)

        def channel(c):
            x = image_ref[at, c * SUB : (c + 1) * SUB, :].reshape(block // fold, fold, SUB, LANE)
            return [x[:, i] for i in range(fold)]

        target = [channel(c) for c in range(CH)]
        energy = [sum(x * x for x in images) for images in zip(*target)]
        product = [sum(s * x for s, x in zip(scaled, images)) for images in zip(*target)]
        tgt_gains = self_gains(grid, grid.swap(energy))
        spread = grid.box(grid.swap(product))
        gains, corrs, rests = [], [], []
        for layer in range(DEPTH):
            gain = [s * t for s, t in zip(gains2[layer], tgt_gains[layer])]
            corr = [(x + BIAS_VAR) * g for x, g in zip(spread, gain)]
            if layer == 0:
                both = [arcsine(x) for x in corr]
            else:
                scale = LATER if layer + 1 < DEPTH else 1.0
                both = [arcsine_inner(x, scale) for x in corr]
            angle = [x for x, _ in both]
            gains.append(gain)
            corrs.append(corr)
            rests.append([x for _, x in both])
            if layer + 1 < DEPTH:
                spread = grid.box(angle)
        sum_of(k, jnp.sum(sum(angle), axis=1))
        slope = [lax.rsqrt(x) for x in rests[-1]]
        carried = [d * (s * x) for d, s, x in zip(decay[-1], slope, corrs[-1])]
        for layer in range(DEPTH - 2, -1, -1):
            grad = grid.box([s * g for s, g in zip(slope, gains[layer + 1])])
            slope = [g * lax.rsqrt(x) for g, x in zip(grad, rests[layer])]
            carried = [
                d * (s * x) + m * y
                for d, s, x, m, y in zip(
                    decay[layer], slope, corrs[layer], slope_of[layer], grid.box(carried)
                )
            ]
        grad = grid.box([s * g for s, g in zip(slope, gains[0])])
        energy = grid.box(carried)
        for c in range(CH):
            for q, x in enumerate(grid.swap(channel(c))):
                plane_ref[to, c, q] = grad[q] * x + energy[q] * double[c][q]
        return carry

    lax.fori_loop(0, image_ref.shape[0] // block, step, 0)


def first_body(
    classes, tgt_hbm, sup_hbm, coef_hbm, lab_hbm,
    image_ref, sup_ref, head_ref, tgt_ref, coef_ref, lab_ref, sems,
):
    pairs = ((tgt_hbm, tgt_ref), (sup_hbm, sup_ref), (coef_hbm, coef_ref), (lab_hbm, lab_ref))
    copies = [pltpu.make_async_copy(a, b, sems.at[k]) for k, (a, b) in enumerate(pairs)]
    for copy in copies:
        copy.start()
    head_ref[...] = jnp.zeros_like(head_ref)
    copies[0].wait()
    image = tgt_ref[...]
    for k in range(image_ref.shape[0]):
        image_ref[k] = image
    for copy in copies[1:]:
        copy.wait()
    labels = lab_ref.shape[-1]
    head_ref[0:1, 0:labels] = coef_ref[pl.ds(lax.axis_index("tgt"), 1), :]
    head_ref[0:1, classes : classes + labels] = lab_ref[...]


def own_body(side, block, own_ref, sup_ref, sum_ref, plane_ref, state_ref):
    grid = Grid(side)
    image = [sup_ref[c * SUB : (c + 1) * SUB, :] for c in range(CH)]
    support = [grid.swap([x] * grid.fold) for x in image]
    gains = self_gains(grid, [sum(x * x for x in rows) for rows in zip(*support)])
    state = (
        [[2.0 * x for x in rows] for rows in support],
        [[2.0 * g for g in gain] for gain in gains],
        [[-(g * g) for g in gain] for gain in gains],
        [[2.0 * (g * g * g) * lax.rsqrt(2.0 - g * g) for g in gain] for gain in gains],
    )
    for part, arrays in enumerate(state):
        for k in range(DEPTH):
            for q in range(grid.fold):
                state_ref[part, k, q] = arrays[k][q]
    state = ([FIRST * x for x in image],) + state

    def sum_of(k, rows):
        for g in range(rows.shape[0]):
            sum_ref[pl.ds(k * rows.shape[0] + g, 1)] = rows[g : g + 1]

    pairs_of(grid, block, own_ref, state, plane_ref, sum_of)


def other_body(
    side, pixels, block, width, oth_ref, sup_ref, state_ref, own_sum_ref, head_ref,
    row_ref, plane_ref, sums,
):
    grid = Grid(side)
    half = oth_ref.shape[0]
    groups = half // grid.fold
    core = lax.axis_index("core")
    for g in range(groups):
        sums[pl.ds(core * groups + g, 1)] = own_sum_ref[g : g + 1]
    state = [[FIRST * sup_ref[c * SUB : (c + 1) * SUB, :] for c in range(CH)]] + [
        [[state_ref[part, layer, q] for q in range(grid.fold)] for layer in range(DEPTH)]
        for part in range(PARTS)
    ]

    def sum_of(k, rows):
        base = (1 - core) * groups + k * rows.shape[0]
        for g in range(rows.shape[0]):
            sums[pl.ds(base + g, 1)] = rows[g : g + 1]

    pairs_of(grid, block, oth_ref, state, plane_ref, sum_of)

    count = 2 * half
    lane = lax.broadcasted_iota(jnp.int32, (LANE, count), 0)
    image = lax.broadcasted_iota(jnp.int32, (LANE, count), 1)
    select = jnp.where(lane // side == image % grid.fold, 1.0, 0.0)
    total = lax.dot_general(
        sums[...],
        select,
        (((1,), (0,)), ((), ())),
        precision=lax.Precision.HIGHEST,
        preferred_element_type=jnp.float32,
    )
    group = lax.broadcasted_iota(jnp.int32, total.shape, 0)
    image = lax.broadcasted_iota(jnp.int32, total.shape, 1)
    total = jnp.sum(
        jnp.where(image // grid.fold == group, total, 0.0), axis=0, keepdims=True
    )
    theta = (WEIGHT_VAR * TWO_PI / pixels) * total + BIAS_VAR
    if width > count:
        theta = jnp.concatenate([theta, jnp.zeros((1, width - count), jnp.float32)], axis=1)
    head = head_ref[...]
    for k in range(count):
        row_ref[k, :, 0:width] = theta
        row_ref[k, :, width:] = head


def final_body(
    side, pixels, row_of, index_of, all_ref, plane0_ref, plane1_ref, grad_ref, res_ref,
    group_weight,
):
    grid = Grid(side)
    fold = grid.fold
    groups = plane0_ref.shape[0]
    count = 2 * groups * fold
    core = lax.axis_index("core")
    me = index_of()
    width, classes = row_of["theta"], row_of["class"]
    theta = all_ref[:, 0, 0:count]
    coeffs = all_ref[:, 0, width : width + classes]
    labels = all_ref[:, 0, width + classes : width + 2 * classes]
    own_coeffs = all_ref[me, :, width : width + classes]
    gram = jnp.sum(coeffs * own_coeffs, axis=1, keepdims=True)
    known = jnp.sum(labels * own_coeffs, axis=1, keepdims=True)
    source = lax.broadcasted_iota(jnp.int32, theta.shape, 0)
    image = lax.broadcasted_iota(jnp.int32, theta.shape, 1)
    terms = theta * gram - jnp.where(source == image, known, 0.0)
    cot = jnp.broadcast_to(jnp.sum(terms, axis=0, keepdims=True), (SUB, count))
    if count % LANE:
        cot = jnp.concatenate([cot, jnp.zeros((SUB, LANE - count % LANE), jnp.float32)], axis=1)
    for g in range(2 * groups):
        tile, lane = divmod(g * fold, LANE)
        part = cot[:, tile * LANE : (tile + 1) * LANE]
        group_weight[g : g + 1] = jnp.take_along_axis(part, grid.place + lane, axis=1)[0:1]

    share = jnp.sum(jnp.where(image == me, theta, 0.0), axis=1, keepdims=True)
    predicted = jnp.sum(share * coeffs, axis=0, keepdims=True)
    own_labels = all_ref[me, :, width + classes : width + 2 * classes]
    res_ref[...] = (predicted - own_labels)[:, 0 : res_ref.shape[-1]]

    block = math.gcd(groups, 4)

    def step(plane_ref, base, k, acc):
        acc = list(acc)
        for g in range(block):
            c = group_weight[pl.ds(base + k * block + g, SUB, stride=0), :]
            for n in range(CH * fold):
                acc[n] = acc[n] + c * plane_ref[k * block + g, n // fold, n % fold]
        return acc

    def both(k, acc):
        acc = step(plane0_ref, core * groups, k, acc)
        return tuple(step(plane1_ref, (1 - core) * groups, k, acc))

    factor = (WEIGHT_VAR * TWO_PI / pixels) * LATER ** (DEPTH - 1) * FIRST
    zero = jnp.zeros((SUB, LANE), jnp.float32)
    acc = lax.fori_loop(0, groups // block, both, (zero,) * (CH * fold))
    for c in range(CH):
        out = None
        for q in range(fold):
            x, shift = acc[c * fold + q], LANE // 2
            while shift >= side:
                x = x + pltpu.roll(x, shift, 1)
                shift //= 2
            out = x if out is None else jnp.where(grid.place == q, x, out)
        grad_ref[c * SUB : (c + 1) * SUB, :] = factor * out


def local(support, coeffs, targets, labels):
    f32 = jnp.float32
    pixels = support.shape[2]
    side = math.isqrt(pixels)
    fold = LANE // side
    chips = lax.axis_size("tgt") * lax.axis_size("row")
    count = 2 * chips
    classes = pl.cdiv(labels.shape[1], LANE) * LANE
    row_of = {"theta": pl.cdiv(count, LANE) * LANE, "class": classes}
    width = row_of["theta"] + 2 * classes
    block = math.gcd(chips, 4 * fold)
    groups = chips // fold
    assert support.shape[0] == 1 and targets.shape[0] == 1
    assert side * side == pixels == SUB * LANE and groups * fold == chips

    vmem = pl.BlockSpec(memory_space=pltpu.VMEM)
    hbm = pl.BlockSpec(memory_space=pltpu.HBM)
    limit = pltpu.CompilerParams(vmem_limit_bytes=16 * 2**20)
    effort = pl.CostEstimate(
        flops=300 * chips * pixels, bytes_accessed=24 * chips * pixels, transcendentals=0
    )

    sup_shape = (CH * SUB, LANE)
    inputs = (targets.reshape(sup_shape), support.reshape(sup_shape), coeffs, labels)
    images, sup, head = pl.pallas_call(
        functools.partial(first_body, classes),
        out_shape=(
            jax.ShapeDtypeStruct((chips,) + sup_shape, f32),
            jax.ShapeDtypeStruct(sup_shape, f32),
            jax.ShapeDtypeStruct((1, 2 * classes), f32),
        ),
        in_specs=[hbm] * 4,
        out_specs=[vmem] * 3,
        scratch_shapes=[
            pltpu.VMEM(sup_shape, f32),
            pltpu.VMEM(coeffs.shape, f32),
            pltpu.VMEM(labels.shape, f32),
            pltpu.SemaphoreType.DMA((4,)),
        ],
        compiler_params=limit,
        name="first",
    )(*(pltpu.with_memory_space_constraint(x, pltpu.HBM) for x in inputs))
    own = lax.all_to_all(images, ("tgt", "row"), 0, 0, tiled=True)
    oth = lax.ppermute(own, "core", [(0, 1), (1, 0)])

    planes = jax.ShapeDtypeStruct((groups, CH, fold, SUB, LANE), f32)
    sums, planes0, state = pl.pallas_call(
        functools.partial(own_body, side, block),
        out_shape=(
            jax.ShapeDtypeStruct((groups, LANE), f32),
            planes,
            jax.ShapeDtypeStruct((PARTS, DEPTH, fold, SUB, LANE), f32),
        ),
        in_specs=[vmem] * 2,
        out_specs=[vmem] * 3,
        compiler_params=limit,
        cost_estimate=effort,
        name="own",
    )(own, sup)
    rows, planes1 = pl.pallas_call(
        functools.partial(other_body, side, pixels, block, row_of["theta"]),
        out_shape=(jax.ShapeDtypeStruct((count, 1, width), f32), planes),
        in_specs=[vmem] * 5,
        out_specs=[vmem] * 2,
        scratch_shapes=[pltpu.VMEM((2 * groups, LANE), f32)],
        compiler_params=limit,
        cost_estimate=effort,
        name="other",
    )(oth, sup, state, sums, head)

    rows = lax.all_to_all(
        rows, ("core", "tgt", "row"), 0, 0, tiled=True
    )

    def index_of():
        tgt, place, core = (lax.axis_index(a) for a in ("tgt", "row", "core"))
        return (core * lax.axis_size("tgt") + tgt) * lax.axis_size("row") + place

    grad, residual = pl.pallas_call(
        functools.partial(final_body, side, pixels, row_of, index_of),
        out_shape=(
            jax.ShapeDtypeStruct(sup.shape, f32),
            jax.ShapeDtypeStruct(labels.shape, f32),
        ),
        in_specs=[vmem] * 3,
        out_specs=[vmem] * 2,
        scratch_shapes=[pltpu.VMEM((2 * groups, LANE), f32)],
        compiler_params=limit,
        name="final",
    )(rows, planes0, planes1)
    return grad.reshape(support.shape), residual


def solution(mesh):
    tgt, sup = mesh.devices.shape
    chips = Mesh(mesh.devices.reshape(tgt, sup // 2, 2), ("tgt", "row", "core"))
    by_support, by_target = ("row", "core", "tgt"), ("tgt", "row", "core")
    return jax.shard_map(
        local,
        mesh=chips,
        in_specs=(
            P(by_support, None, None),
            P(("row", "core"), None),
            P(by_target, None, None),
            P(by_target, None),
        ),
        out_specs=(P(by_support, None, None), P(by_target, None)),
        check_vma=False,
    )
```

```python
import functools
import math

import jax
import jax.numpy as jnp
from jax import lax
from jax.experimental import pallas as pl
from jax.experimental.pallas import tpu as pltpu
from jax.sharding import Mesh
from jax.sharding import PartitionSpec as P

WEIGHT_VAR = 1.6
BIAS_VAR = 0.1
DEPTH = 3
CH = 3
SUB = 8
LANE = 128
TWO_PI = 2.0 / math.pi
PARTS = 4
FIRST = WEIGHT_VAR / (9 * CH)
LATER = WEIGHT_VAR * TWO_PI / 9

NEAR = (1.6666752422e-1, 7.4953002686e-2, 4.5470025998e-2, 2.4181311049e-2, 4.2163199048e-2)
WIDE = (
    1.0,
    0.16666266322135925,
    0.07520359754562378,
    0.04114901274442673,
    0.058932434767484665,
    -0.10370756685733795,
    0.3290194272994995,
    -0.39874982833862305,
    0.2500518262386322,
)
HALF = (
    1.0000000202678234,
    0.1666621810142767,
    0.07516158417922122,
    0.042482407794996346,
    0.04384003568012658,
    -0.018689176226557736,
    0.07216594689625302,
)


def horner(z, coefficients, scale=1.0):
    result = scale * coefficients[-1]
    for value in coefficients[-2::-1]:
        result = result * z + scale * value
    return result


def arcsine(x):
    a = jnp.abs(x)
    large, negative = a > 0.5, x < 0.0
    left = 1.0 - a
    z = jnp.where(large, 0.5 * left, x * x)
    root = (2.0 * left) * lax.rsqrt(2.0 * left)
    t = jnp.where(large, jnp.where(negative, root, -root), x)
    right = LATER * 0.5 * math.pi
    offset = jnp.where(large, jnp.where(negative, -right, right), 0.0)
    return offset + t * (LATER + z * horner(z, NEAR, LATER)), left * (1.0 + a)


def arcsine_inner(x, scale):
    z = x * x
    return x * horner(z, WIDE, scale), 1.0 - z


def chip_order(tgts, rows):
    return [(t, (k + 1) % rows) for t in reversed(range(tgts)) for k in range(rows)]


class Grid:
    def __init__(self, side):
        lane = lax.broadcasted_iota(jnp.int32, (SUB, LANE), 1)
        sub = lax.broadcasted_iota(jnp.int32, (SUB, LANE), 0)
        self.side, self.fold = side, LANE // side
        column = lane % side
        self.place = lane // side
        self.not_left, self.not_right = column != 0, column != side - 1
        self.not_top, self.not_bottom = sub != 0, sub != SUB - 1

    def neighbours(self):
        across = jnp.where(self.not_left, 1.0, 0.0) + jnp.where(self.not_right, 2.0, 1.0)
        rows = [across * 3.0] * self.fold
        rows[0] = across * jnp.where(self.not_top, 3.0, 2.0)
        rows[-1] = across * jnp.where(self.not_bottom, 3.0, 2.0)
        return rows

    def swap(self, arrays):
        arrays, step = list(arrays), 1
        while step < self.fold:
            low = (self.place // step) % 2 == 0
            shift = step * self.side
            for i in range(self.fold):
                if i & step == 0:
                    a, b = arrays[i], arrays[i + step]
                    axis = a.ndim - 1
                    arrays[i] = jnp.where(low, a, pltpu.roll(b, shift, axis))
                    arrays[i + step] = jnp.where(low, pltpu.roll(a, LANE - shift, axis), b)
            step *= 2
        return arrays

    def box(self, rows):
        h = []
        for x in rows:
            axis = x.ndim - 1
            h.append(
                x
                + jnp.where(self.not_left, pltpu.roll(x, 1, axis), 0.0)
                + jnp.where(self.not_right, pltpu.roll(x, LANE - 1, axis), 0.0)
            )
        axis = rows[0].ndim - 2
        above = jnp.where(self.not_top, pltpu.roll(h[-1], 1, axis), 0.0)
        below = jnp.where(self.not_bottom, pltpu.roll(h[0], SUB - 1, axis), 0.0)
        ring = [above] + h + [below]
        pairs = [ring[k] + ring[k + 1] for k in range(0, len(ring), 2)]
        out = []
        for q in range(self.fold):
            if q % 2 == 0:
                out.append(pairs[q // 2] + ring[q + 2])
            else:
                out.append(ring[q] + pairs[(q + 1) // 2])
        return out


def self_gains(grid, energy):
    start = 1.0 + 2.0 * BIAS_VAR
    gain = [lax.rsqrt((2.0 * FIRST) * x + start) for x in grid.box(energy)]
    gains = [gain]
    most = [(LATER * math.pi) * n + start for n in grid.neighbours()]
    powers = [c * 0.5**k for k, c in enumerate(HALF)]
    for _ in range(DEPTH - 1):
        less = [g * horner(g * g, powers, 4.0 * LATER * math.sqrt(0.5)) for g in gain]
        gain = [lax.rsqrt(m - x) for m, x in zip(most, grid.box(less))]
        gains.append(gain)
    return gains


def pairs_of(grid, block, image_ref, state, plane_ref, sum_of):
    scaled, double, gains2, decay, slope_of = state
    fold = grid.fold

    def step(k, carry):
        at = pl.ds(k * block, block)
        to = pl.ds(k * (block // fold), block // fold)

        def channel(c):
            x = image_ref[at, c * SUB : (c + 1) * SUB, :].reshape(block // fold, fold, SUB, LANE)
            return [x[:, i] for i in range(fold)]

        target = [channel(c) for c in range(CH)]
        energy = [sum(x * x for x in images) for images in zip(*target)]
        product = [sum(s * x for s, x in zip(scaled, images)) for images in zip(*target)]
        tgt_gains = self_gains(grid, grid.swap(energy))
        spread = grid.box(grid.swap(product))
        gains, corrs, rests = [], [], []
        for layer in range(DEPTH):
            gain = [s * t for s, t in zip(gains2[layer], tgt_gains[layer])]
            corr = [(x + BIAS_VAR) * g for x, g in zip(spread, gain)]
            if layer == 0:
                both = [arcsine(x) for x in corr]
            else:
                scale = LATER if layer + 1 < DEPTH else 1.0
                both = [arcsine_inner(x, scale) for x in corr]
            angle = [x for x, _ in both]
            gains.append(gain)
            corrs.append(corr)
            rests.append([x for _, x in both])
            if layer + 1 < DEPTH:
                spread = grid.box(angle)
        sum_of(k, jnp.sum(sum(angle), axis=1))
        slope = [lax.rsqrt(x) for x in rests[-1]]
        carried = [d * (s * x) for d, s, x in zip(decay[-1], slope, corrs[-1])]
        for layer in range(DEPTH - 2, -1, -1):
            grad = grid.box([s * g for s, g in zip(slope, gains[layer + 1])])
            slope = [g * lax.rsqrt(x) for g, x in zip(grad, rests[layer])]
            carried = [
                d * (s * x) + m * y
                for d, s, x, m, y in zip(
                    decay[layer], slope, corrs[layer], slope_of[layer], grid.box(carried)
                )
            ]
        grad = grid.box([s * g for s, g in zip(slope, gains[0])])
        energy = grid.box(carried)
        for c in range(CH):
            for q, x in enumerate(grid.swap(channel(c))):
                plane_ref[to, c, q] = grad[q] * x + energy[q] * double[c][q]
        return carry

    lax.fori_loop(0, image_ref.shape[0] // block, step, 0)


def first_body(
    classes, tgt_hbm, sup_hbm, coef_hbm, lab_hbm,
    image_ref, sup_ref, head_ref, tgt_ref, coef_ref, lab_ref, sems,
):
    pairs = ((tgt_hbm, tgt_ref), (sup_hbm, sup_ref), (coef_hbm, coef_ref), (lab_hbm, lab_ref))
    copies = [pltpu.make_async_copy(a, b, sems.at[k]) for k, (a, b) in enumerate(pairs)]
    for copy in copies:
        copy.start()
    head_ref[...] = jnp.zeros_like(head_ref)
    copies[0].wait()
    image = tgt_ref[...]
    for k in range(image_ref.shape[0]):
        image_ref[k] = image
    for copy in copies[1:]:
        copy.wait()
    labels = lab_ref.shape[-1]
    head_ref[0:1, 0:labels] = coef_ref[pl.ds(lax.axis_index("tgt"), 1), :]
    head_ref[0:1, classes : classes + labels] = lab_ref[...]


def own_body(side, block, own_ref, sup_ref, sum_ref, plane_ref, state_ref):
    grid = Grid(side)
    image = [sup_ref[c * SUB : (c + 1) * SUB, :] for c in range(CH)]
    support = [grid.swap([x] * grid.fold) for x in image]
    gains = self_gains(grid, [sum(x * x for x in rows) for rows in zip(*support)])
    state = (
        [[2.0 * x for x in rows] for rows in support],
        [[2.0 * g for g in gain] for gain in gains],
        [[-(g * g) for g in gain] for gain in gains],
        [[2.0 * (g * g * g) * lax.rsqrt(2.0 - g * g) for g in gain] for gain in gains],
    )
    for part, arrays in enumerate(state):
        for k in range(DEPTH):
            for q in range(grid.fold):
                state_ref[part, k, q] = arrays[k][q]
    state = ([FIRST * x for x in image],) + state

    def sum_of(k, rows):
        for g in range(rows.shape[0]):
            sum_ref[pl.ds(k * rows.shape[0] + g, 1)] = rows[g : g + 1]

    pairs_of(grid, block, own_ref, state, plane_ref, sum_of)


def other_body(
    side, pixels, block, width, oth_ref, sup_ref, state_ref, own_sum_ref, head_ref,
    row_ref, plane_ref, sums,
):
    grid = Grid(side)
    half = oth_ref.shape[0]
    groups = half // grid.fold
    core = lax.axis_index("core")
    for g in range(groups):
        sums[pl.ds(core * groups + g, 1)] = own_sum_ref[g : g + 1]
    state = [[FIRST * sup_ref[c * SUB : (c + 1) * SUB, :] for c in range(CH)]] + [
        [[state_ref[part, layer, q] for q in range(grid.fold)] for layer in range(DEPTH)]
        for part in range(PARTS)
    ]

    def sum_of(k, rows):
        base = (1 - core) * groups + k * rows.shape[0]
        for g in range(rows.shape[0]):
            sums[pl.ds(base + g, 1)] = rows[g : g + 1]

    pairs_of(grid, block, oth_ref, state, plane_ref, sum_of)

    count = 2 * half
    lane = lax.broadcasted_iota(jnp.int32, (LANE, count), 0)
    image = lax.broadcasted_iota(jnp.int32, (LANE, count), 1)
    select = jnp.where(lane // side == image % grid.fold, 1.0, 0.0)
    total = lax.dot_general(
        sums[...],
        select,
        (((1,), (0,)), ((), ())),
        precision=lax.Precision.HIGHEST,
        preferred_element_type=jnp.float32,
    )
    group = lax.broadcasted_iota(jnp.int32, total.shape, 0)
    image = lax.broadcasted_iota(jnp.int32, total.shape, 1)
    total = jnp.sum(
        jnp.where(image // grid.fold == group, total, 0.0), axis=0, keepdims=True
    )
    theta = (WEIGHT_VAR * TWO_PI / pixels) * total + BIAS_VAR
    if width > count:
        theta = jnp.concatenate([theta, jnp.zeros((1, width - count), jnp.float32)], axis=1)
    head = head_ref[...]
    for k in range(count):
        row_ref[k, :, 0:width] = theta
        row_ref[k, :, width:] = head


def final_body(
    side, pixels, row_of, index_of, all_ref, plane0_ref, plane1_ref, grad_ref, res_ref,
    group_weight,
):
    grid = Grid(side)
    fold = grid.fold
    groups = plane0_ref.shape[0]
    count = 2 * groups * fold
    core = lax.axis_index("core")
    me = index_of()
    width, classes = row_of["theta"], row_of["class"]
    theta = all_ref[:, 0, 0:count]
    coeffs = all_ref[:, 0, width : width + classes]
    labels = all_ref[:, 0, width + classes : width + 2 * classes]
    own_coeffs = all_ref[me, :, width : width + classes]
    gram = jnp.sum(coeffs * own_coeffs, axis=1, keepdims=True)
    known = jnp.sum(labels * own_coeffs, axis=1, keepdims=True)
    source = lax.broadcasted_iota(jnp.int32, theta.shape, 0)
    image = lax.broadcasted_iota(jnp.int32, theta.shape, 1)
    terms = theta * gram - jnp.where(source == image, known, 0.0)
    cot = jnp.broadcast_to(jnp.sum(terms, axis=0, keepdims=True), (SUB, count))
    if count % LANE:
        cot = jnp.concatenate([cot, jnp.zeros((SUB, LANE - count % LANE), jnp.float32)], axis=1)
    for g in range(2 * groups):
        tile, lane = divmod(g * fold, LANE)
        part = cot[:, tile * LANE : (tile + 1) * LANE]
        group_weight[g : g + 1] = jnp.take_along_axis(part, grid.place + lane, axis=1)[0:1]

    share = jnp.sum(jnp.where(image == me, theta, 0.0), axis=1, keepdims=True)
    predicted = jnp.sum(share * coeffs, axis=0, keepdims=True)
    own_labels = all_ref[me, :, width + classes : width + 2 * classes]
    res_ref[...] = (predicted - own_labels)[:, 0 : res_ref.shape[-1]]

    block = math.gcd(groups, 4)

    def step(plane_ref, base, k, acc):
        acc = list(acc)
        for g in range(block):
            c = group_weight[pl.ds(base + k * block + g, SUB, stride=0), :]
            for n in range(CH * fold):
                acc[n] = acc[n] + c * plane_ref[k * block + g, n // fold, n % fold]
        return acc

    def both(k, acc):
        acc = step(plane0_ref, core * groups, k, acc)
        return tuple(step(plane1_ref, (1 - core) * groups, k, acc))

    factor = (WEIGHT_VAR * TWO_PI / pixels) * LATER ** (DEPTH - 1) * FIRST
    zero = jnp.zeros((SUB, LANE), jnp.float32)
    acc = lax.fori_loop(0, groups // block, both, (zero,) * (CH * fold))
    for c in range(CH):
        out = None
        for q in range(fold):
            x, shift = acc[c * fold + q], LANE // 2
            while shift >= side:
                x = x + pltpu.roll(x, shift, 1)
                shift //= 2
            out = x if out is None else jnp.where(grid.place == q, x, out)
        grad_ref[c * SUB : (c + 1) * SUB, :] = factor * out


def local(support, coeffs, targets, labels):
    f32 = jnp.float32
    pixels = support.shape[2]
    side = math.isqrt(pixels)
    fold = LANE // side
    chips = lax.axis_size("tgt") * lax.axis_size("row")
    count = 2 * chips
    classes = pl.cdiv(labels.shape[1], LANE) * LANE
    row_of = {"theta": pl.cdiv(count, LANE) * LANE, "class": classes}
    width = row_of["theta"] + 2 * classes
    block = math.gcd(chips, 4 * fold)
    groups = chips // fold
    assert support.shape[0] == 1 and targets.shape[0] == 1
    assert side * side == pixels == SUB * LANE and groups * fold == chips

    vmem = pl.BlockSpec(memory_space=pltpu.VMEM)
    hbm = pl.BlockSpec(memory_space=pltpu.HBM)
    limit = pltpu.CompilerParams(vmem_limit_bytes=16 * 2**20)
    effort = pl.CostEstimate(
        flops=300 * chips * pixels, bytes_accessed=24 * chips * pixels, transcendentals=0
    )

    sup_shape = (CH * SUB, LANE)
    inputs = (targets.reshape(sup_shape), support.reshape(sup_shape), coeffs, labels)
    images, sup, head = pl.pallas_call(
        functools.partial(first_body, classes),
        out_shape=(
            jax.ShapeDtypeStruct((chips,) + sup_shape, f32),
            jax.ShapeDtypeStruct(sup_shape, f32),
            jax.ShapeDtypeStruct((1, 2 * classes), f32),
        ),
        in_specs=[hbm] * 4,
        out_specs=[vmem] * 3,
        scratch_shapes=[
            pltpu.VMEM(sup_shape, f32),
            pltpu.VMEM(coeffs.shape, f32),
            pltpu.VMEM(labels.shape, f32),
            pltpu.SemaphoreType.DMA((4,)),
        ],
        compiler_params=limit,
        name="first",
    )(*(pltpu.with_memory_space_constraint(x, pltpu.HBM) for x in inputs))
    axes = ("tgt", "row", "core")
    tgts, rows = lax.axis_size("tgt"), lax.axis_size("row")
    order = chip_order(tgts, rows)
    halves = [[(t * rows + r) * 2 + core for t, r in order] for core in range(2)]
    own = lax.all_to_all(images, axes, 0, 0, axis_index_groups=halves, tiled=True)
    oth = lax.ppermute(own, "core", [(0, 1), (1, 0)])

    planes = jax.ShapeDtypeStruct((groups, CH, fold, SUB, LANE), f32)
    sums, planes0, state = pl.pallas_call(
        functools.partial(own_body, side, block),
        out_shape=(
            jax.ShapeDtypeStruct((groups, LANE), f32),
            planes,
            jax.ShapeDtypeStruct((PARTS, DEPTH, fold, SUB, LANE), f32),
        ),
        in_specs=[vmem] * 2,
        out_specs=[vmem] * 3,
        compiler_params=limit,
        cost_estimate=effort,
        name="own",
    )(own, sup)
    theta_rows, planes1 = pl.pallas_call(
        functools.partial(other_body, side, pixels, block, row_of["theta"]),
        out_shape=(jax.ShapeDtypeStruct((count, 1, width), f32), planes),
        in_specs=[vmem] * 5,
        out_specs=[vmem] * 2,
        scratch_shapes=[pltpu.VMEM((2 * groups, LANE), f32)],
        compiler_params=limit,
        cost_estimate=effort,
        name="other",
    )(oth, sup, state, sums, head)

    theta_rows = lax.all_to_all(
        theta_rows, axes, 0, 0, axis_index_groups=[halves[0] + halves[1]], tiled=True
    )

    def index_of():
        t, r, core = (lax.axis_index(a) for a in axes)
        return core * chips + (tgts - 1 - t) * rows + lax.rem(r + rows - 1, rows)

    grad, residual = pl.pallas_call(
        functools.partial(final_body, side, pixels, row_of, index_of),
        out_shape=(
            jax.ShapeDtypeStruct(sup.shape, f32),
            jax.ShapeDtypeStruct(labels.shape, f32),
        ),
        in_specs=[vmem] * 3,
        out_specs=[vmem] * 2,
        scratch_shapes=[pltpu.VMEM((2 * groups, LANE), f32)],
        compiler_params=limit,
        name="final",
    )(theta_rows, planes0, planes1)
    return grad.reshape(support.shape), residual


def solution(mesh):
    tgt, sup = mesh.devices.shape
    chips = Mesh(mesh.devices.reshape(tgt, sup // 2, 2), ("tgt", "row", "core"))
    by_support, by_target = ("row", "core", "tgt"), ("tgt", "row", "core")
    return jax.shard_map(
        local,
        mesh=chips,
        in_specs=(
            P(by_support, None, None),
            P(("row", "core"), None),
            P(by_target, None, None),
            P(by_target, None),
        ),
        out_specs=(P(by_support, None, None), P(by_target, None)),
        check_vma=False,
    )
```

```python
import functools
import math

import jax
import jax.numpy as jnp
from jax import lax
from jax.experimental import pallas as pl
from jax.experimental.pallas import tpu as pltpu
from jax.sharding import Mesh
from jax.sharding import PartitionSpec as P

WEIGHT_VAR = 1.6
BIAS_VAR = 0.1
DEPTH = 3
CH = 3
SUB = 8
LANE = 128
TWO_PI = 2.0 / math.pi
PARTS = 4
FIRST = WEIGHT_VAR / (9 * CH)
LATER = WEIGHT_VAR * TWO_PI / 9

NEAR = (1.6666752422e-1, 7.4953002686e-2, 4.5470025998e-2, 2.4181311049e-2, 4.2163199048e-2)
WIDE = (
    1.0,
    0.16666266322135925,
    0.07520359754562378,
    0.04114901274442673,
    0.058932434767484665,
    -0.10370756685733795,
    0.3290194272994995,
    -0.39874982833862305,
    0.2500518262386322,
)
HALF = (
    1.0000000202678234,
    0.1666621810142767,
    0.07516158417922122,
    0.042482407794996346,
    0.04384003568012658,
    -0.018689176226557736,
    0.07216594689625302,
)


def horner(z, coefficients, scale=1.0):
    result = scale * coefficients[-1]
    for value in coefficients[-2::-1]:
        result = result * z + scale * value
    return result


def arcsine(x):
    a = jnp.abs(x)
    large, negative = a > 0.5, x < 0.0
    left = 1.0 - a
    z = jnp.where(large, 0.5 * left, x * x)
    root = (2.0 * left) * lax.rsqrt(2.0 * left)
    t = jnp.where(large, jnp.where(negative, root, -root), x)
    right = LATER * 0.5 * math.pi
    offset = jnp.where(large, jnp.where(negative, -right, right), 0.0)
    return offset + t * (LATER + z * horner(z, NEAR, LATER)), left * (1.0 + a)


def arcsine_inner(x, scale):
    z = x * x
    return x * horner(z, WIDE, scale), 1.0 - z


def chip_order(tgts, rows):
    return [(t, (1 + rows - k) % rows) for t in reversed(range(tgts)) for k in range(rows)]


class Grid:
    def __init__(self, side):
        lane = lax.broadcasted_iota(jnp.int32, (SUB, LANE), 1)
        sub = lax.broadcasted_iota(jnp.int32, (SUB, LANE), 0)
        self.side, self.fold = side, LANE // side
        column = lane % side
        self.place = lane // side
        self.not_left, self.not_right = column != 0, column != side - 1
        self.not_top, self.not_bottom = sub != 0, sub != SUB - 1

    def neighbours(self):
        across = jnp.where(self.not_left, 1.0, 0.0) + jnp.where(self.not_right, 2.0, 1.0)
        rows = [across * 3.0] * self.fold
        rows[0] = across * jnp.where(self.not_top, 3.0, 2.0)
        rows[-1] = across * jnp.where(self.not_bottom, 3.0, 2.0)
        return rows

    def swap(self, arrays):
        arrays, step = list(arrays), 1
        while step < self.fold:
            low = (self.place // step) % 2 == 0
            shift = step * self.side
            for i in range(self.fold):
                if i & step == 0:
                    a, b = arrays[i], arrays[i + step]
                    axis = a.ndim - 1
                    arrays[i] = jnp.where(low, a, pltpu.roll(b, shift, axis))
                    arrays[i + step] = jnp.where(low, pltpu.roll(a, LANE - shift, axis), b)
            step *= 2
        return arrays

    def box(self, rows):
        h = []
        for x in rows:
            axis = x.ndim - 1
            h.append(
                x
                + jnp.where(self.not_left, pltpu.roll(x, 1, axis), 0.0)
                + jnp.where(self.not_right, pltpu.roll(x, LANE - 1, axis), 0.0)
            )
        axis = rows[0].ndim - 2
        above = jnp.where(self.not_top, pltpu.roll(h[-1], 1, axis), 0.0)
        below = jnp.where(self.not_bottom, pltpu.roll(h[0], SUB - 1, axis), 0.0)
        ring = [above] + h + [below]
        pairs = [ring[k] + ring[k + 1] for k in range(0, len(ring), 2)]
        out = []
        for q in range(self.fold):
            if q % 2 == 0:
                out.append(pairs[q // 2] + ring[q + 2])
            else:
                out.append(ring[q] + pairs[(q + 1) // 2])
        return out


def self_gains(grid, energy):
    start = 1.0 + 2.0 * BIAS_VAR
    gain = [lax.rsqrt((2.0 * FIRST) * x + start) for x in grid.box(energy)]
    gains = [gain]
    most = [(LATER * math.pi) * n + start for n in grid.neighbours()]
    powers = [c * 0.5**k for k, c in enumerate(HALF)]
    for _ in range(DEPTH - 1):
        less = [g * horner(g * g, powers, 4.0 * LATER * math.sqrt(0.5)) for g in gain]
        gain = [lax.rsqrt(m - x) for m, x in zip(most, grid.box(less))]
        gains.append(gain)
    return gains


def pairs_of(grid, block, image_ref, state, plane_ref, sum_of):
    scaled, double, gains2, decay, slope_of = state
    fold = grid.fold

    def step(k, carry):
        at = pl.ds(k * block, block)
        to = pl.ds(k * (block // fold), block // fold)

        def channel(c):
            x = image_ref[at, c * SUB : (c + 1) * SUB, :].reshape(block // fold, fold, SUB, LANE)
            return [x[:, i] for i in range(fold)]

        target = [channel(c) for c in range(CH)]
        energy = [sum(x * x for x in images) for images in zip(*target)]
        product = [sum(s * x for s, x in zip(scaled, images)) for images in zip(*target)]
        tgt_gains = self_gains(grid, grid.swap(energy))
        spread = grid.box(grid.swap(product))
        gains, corrs, rests = [], [], []
        for layer in range(DEPTH):
            gain = [s * t for s, t in zip(gains2[layer], tgt_gains[layer])]
            corr = [(x + BIAS_VAR) * g for x, g in zip(spread, gain)]
            if layer == 0:
                both = [arcsine(x) for x in corr]
            else:
                scale = LATER if layer + 1 < DEPTH else 1.0
                both = [arcsine_inner(x, scale) for x in corr]
            angle = [x for x, _ in both]
            gains.append(gain)
            corrs.append(corr)
            rests.append([x for _, x in both])
            if layer + 1 < DEPTH:
                spread = grid.box(angle)
        sum_of(k, jnp.sum(sum(angle), axis=1))
        slope = [lax.rsqrt(x) for x in rests[-1]]
        carried = [d * (s * x) for d, s, x in zip(decay[-1], slope, corrs[-1])]
        for layer in range(DEPTH - 2, -1, -1):
            grad = grid.box([s * g for s, g in zip(slope, gains[layer + 1])])
            slope = [g * lax.rsqrt(x) for g, x in zip(grad, rests[layer])]
            carried = [
                d * (s * x) + m * y
                for d, s, x, m, y in zip(
                    decay[layer], slope, corrs[layer], slope_of[layer], grid.box(carried)
                )
            ]
        grad = grid.box([s * g for s, g in zip(slope, gains[0])])
        energy = grid.box(carried)
        for c in range(CH):
            for q, x in enumerate(grid.swap(channel(c))):
                plane_ref[to, c, q] = grad[q] * x + energy[q] * double[c][q]
        return carry

    lax.fori_loop(0, image_ref.shape[0] // block, step, 0)


def first_body(
    classes, tgt_hbm, sup_hbm, coef_hbm, lab_hbm,
    image_ref, sup_ref, head_ref, tgt_ref, coef_ref, lab_ref, sems,
):
    pairs = ((tgt_hbm, tgt_ref), (sup_hbm, sup_ref), (coef_hbm, coef_ref), (lab_hbm, lab_ref))
    copies = [pltpu.make_async_copy(a, b, sems.at[k]) for k, (a, b) in enumerate(pairs)]
    for copy in copies:
        copy.start()
    head_ref[...] = jnp.zeros_like(head_ref)
    copies[0].wait()
    image = tgt_ref[...]
    for k in range(image_ref.shape[0]):
        image_ref[k] = image
    for copy in copies[1:]:
        copy.wait()
    labels = lab_ref.shape[-1]
    head_ref[0:1, 0:labels] = coef_ref[pl.ds(lax.axis_index("tgt"), 1), :]
    head_ref[0:1, classes : classes + labels] = lab_ref[...]


def own_body(side, block, own_ref, sup_ref, sum_ref, plane_ref, state_ref):
    grid = Grid(side)
    image = [sup_ref[c * SUB : (c + 1) * SUB, :] for c in range(CH)]
    support = [grid.swap([x] * grid.fold) for x in image]
    gains = self_gains(grid, [sum(x * x for x in rows) for rows in zip(*support)])
    state = (
        [[2.0 * x for x in rows] for rows in support],
        [[2.0 * g for g in gain] for gain in gains],
        [[-(g * g) for g in gain] for gain in gains],
        [[2.0 * (g * g * g) * lax.rsqrt(2.0 - g * g) for g in gain] for gain in gains],
    )
    for part, arrays in enumerate(state):
        for k in range(DEPTH):
            for q in range(grid.fold):
                state_ref[part, k, q] = arrays[k][q]
    state = ([FIRST * x for x in image],) + state

    def sum_of(k, rows):
        for g in range(rows.shape[0]):
            sum_ref[pl.ds(k * rows.shape[0] + g, 1)] = rows[g : g + 1]

    pairs_of(grid, block, own_ref, state, plane_ref, sum_of)


def other_body(
    side, pixels, block, width, oth_ref, sup_ref, state_ref, own_sum_ref, head_ref,
    row_ref, plane_ref, sums,
):
    grid = Grid(side)
    half = oth_ref.shape[0]
    groups = half // grid.fold
    core = lax.axis_index("core")
    for g in range(groups):
        sums[pl.ds(core * groups + g, 1)] = own_sum_ref[g : g + 1]
    state = [[FIRST * sup_ref[c * SUB : (c + 1) * SUB, :] for c in range(CH)]] + [
        [[state_ref[part, layer, q] for q in range(grid.fold)] for layer in range(DEPTH)]
        for part in range(PARTS)
    ]

    def sum_of(k, rows):
        base = (1 - core) * groups + k * rows.shape[0]
        for g in range(rows.shape[0]):
            sums[pl.ds(base + g, 1)] = rows[g : g + 1]

    pairs_of(grid, block, oth_ref, state, plane_ref, sum_of)

    count = 2 * half
    lane = lax.broadcasted_iota(jnp.int32, (LANE, count), 0)
    image = lax.broadcasted_iota(jnp.int32, (LANE, count), 1)
    select = jnp.where(lane // side == image % grid.fold, 1.0, 0.0)
    total = lax.dot_general(
        sums[...],
        select,
        (((1,), (0,)), ((), ())),
        precision=lax.Precision.HIGHEST,
        preferred_element_type=jnp.float32,
    )
    group = lax.broadcasted_iota(jnp.int32, total.shape, 0)
    image = lax.broadcasted_iota(jnp.int32, total.shape, 1)
    total = jnp.sum(
        jnp.where(image // grid.fold == group, total, 0.0), axis=0, keepdims=True
    )
    theta = (WEIGHT_VAR * TWO_PI / pixels) * total + BIAS_VAR
    if width > count:
        theta = jnp.concatenate([theta, jnp.zeros((1, width - count), jnp.float32)], axis=1)
    head = head_ref[...]
    for k in range(count):
        row_ref[k, :, 0:width] = theta
        row_ref[k, :, width:] = head


def final_body(
    side, pixels, row_of, index_of, all_ref, plane0_ref, plane1_ref, grad_ref, res_ref,
    group_weight,
):
    grid = Grid(side)
    fold = grid.fold
    groups = plane0_ref.shape[0]
    count = 2 * groups * fold
    core = lax.axis_index("core")
    me = index_of()
    width, classes = row_of["theta"], row_of["class"]
    theta = all_ref[:, 0, 0:count]
    coeffs = all_ref[:, 0, width : width + classes]
    labels = all_ref[:, 0, width + classes : width + 2 * classes]
    own_coeffs = all_ref[me, :, width : width + classes]
    gram = jnp.sum(coeffs * own_coeffs, axis=1, keepdims=True)
    known = jnp.sum(labels * own_coeffs, axis=1, keepdims=True)
    source = lax.broadcasted_iota(jnp.int32, theta.shape, 0)
    image = lax.broadcasted_iota(jnp.int32, theta.shape, 1)
    terms = theta * gram - jnp.where(source == image, known, 0.0)
    cot = jnp.broadcast_to(jnp.sum(terms, axis=0, keepdims=True), (SUB, count))
    if count % LANE:
        cot = jnp.concatenate([cot, jnp.zeros((SUB, LANE - count % LANE), jnp.float32)], axis=1)
    for g in range(2 * groups):
        tile, lane = divmod(g * fold, LANE)
        part = cot[:, tile * LANE : (tile + 1) * LANE]
        group_weight[g : g + 1] = jnp.take_along_axis(part, grid.place + lane, axis=1)[0:1]

    share = jnp.sum(jnp.where(image == me, theta, 0.0), axis=1, keepdims=True)
    predicted = jnp.sum(share * coeffs, axis=0, keepdims=True)
    own_labels = all_ref[me, :, width + classes : width + 2 * classes]
    res_ref[...] = (predicted - own_labels)[:, 0 : res_ref.shape[-1]]

    block = math.gcd(groups, 4)

    def step(plane_ref, base, k, acc):
        acc = list(acc)
        for g in range(block):
            c = group_weight[pl.ds(base + k * block + g, SUB, stride=0), :]
            for n in range(CH * fold):
                acc[n] = acc[n] + c * plane_ref[k * block + g, n // fold, n % fold]
        return acc

    def both(k, acc):
        acc = step(plane0_ref, core * groups, k, acc)
        return tuple(step(plane1_ref, (1 - core) * groups, k, acc))

    factor = (WEIGHT_VAR * TWO_PI / pixels) * LATER ** (DEPTH - 1) * FIRST
    zero = jnp.zeros((SUB, LANE), jnp.float32)
    acc = lax.fori_loop(0, groups // block, both, (zero,) * (CH * fold))
    for c in range(CH):
        out = None
        for q in range(fold):
            x, shift = acc[c * fold + q], LANE // 2
            while shift >= side:
                x = x + pltpu.roll(x, shift, 1)
                shift //= 2
            out = x if out is None else jnp.where(grid.place == q, x, out)
        grad_ref[c * SUB : (c + 1) * SUB, :] = factor * out


def local(support, coeffs, targets, labels):
    f32 = jnp.float32
    pixels = support.shape[2]
    side = math.isqrt(pixels)
    fold = LANE // side
    chips = lax.axis_size("tgt") * lax.axis_size("row")
    count = 2 * chips
    classes = pl.cdiv(labels.shape[1], LANE) * LANE
    row_of = {"theta": pl.cdiv(count, LANE) * LANE, "class": classes}
    width = row_of["theta"] + 2 * classes
    block = math.gcd(chips, 4 * fold)
    groups = chips // fold
    assert support.shape[0] == 1 and targets.shape[0] == 1
    assert side * side == pixels == SUB * LANE and groups * fold == chips

    vmem = pl.BlockSpec(memory_space=pltpu.VMEM)
    hbm = pl.BlockSpec(memory_space=pltpu.HBM)
    limit = pltpu.CompilerParams(vmem_limit_bytes=16 * 2**20)
    effort = pl.CostEstimate(
        flops=300 * chips * pixels, bytes_accessed=24 * chips * pixels, transcendentals=0
    )

    sup_shape = (CH * SUB, LANE)
    inputs = (targets.reshape(sup_shape), support.reshape(sup_shape), coeffs, labels)
    images, sup, head = pl.pallas_call(
        functools.partial(first_body, classes),
        out_shape=(
            jax.ShapeDtypeStruct((chips,) + sup_shape, f32),
            jax.ShapeDtypeStruct(sup_shape, f32),
            jax.ShapeDtypeStruct((1, 2 * classes), f32),
        ),
        in_specs=[hbm] * 4,
        out_specs=[vmem] * 3,
        scratch_shapes=[
            pltpu.VMEM(sup_shape, f32),
            pltpu.VMEM(coeffs.shape, f32),
            pltpu.VMEM(labels.shape, f32),
            pltpu.SemaphoreType.DMA((4,)),
        ],
        compiler_params=limit,
        name="first",
    )(*(pltpu.with_memory_space_constraint(x, pltpu.HBM) for x in inputs))
    axes = ("tgt", "row", "core")
    tgts, rows = lax.axis_size("tgt"), lax.axis_size("row")
    order = chip_order(tgts, rows)
    halves = [[(t * rows + r) * 2 + core for t, r in order] for core in range(2)]
    own = lax.all_to_all(images, axes, 0, 0, axis_index_groups=halves, tiled=True)
    oth = lax.ppermute(own, "core", [(0, 1), (1, 0)])

    planes = jax.ShapeDtypeStruct((groups, CH, fold, SUB, LANE), f32)
    sums, planes0, state = pl.pallas_call(
        functools.partial(own_body, side, block),
        out_shape=(
            jax.ShapeDtypeStruct((groups, LANE), f32),
            planes,
            jax.ShapeDtypeStruct((PARTS, DEPTH, fold, SUB, LANE), f32),
        ),
        in_specs=[vmem] * 2,
        out_specs=[vmem] * 3,
        compiler_params=limit,
        cost_estimate=effort,
        name="own",
    )(own, sup)
    theta_rows, planes1 = pl.pallas_call(
        functools.partial(other_body, side, pixels, block, row_of["theta"]),
        out_shape=(jax.ShapeDtypeStruct((count, 1, width), f32), planes),
        in_specs=[vmem] * 5,
        out_specs=[vmem] * 2,
        scratch_shapes=[pltpu.VMEM((2 * groups, LANE), f32)],
        compiler_params=limit,
        cost_estimate=effort,
        name="other",
    )(oth, sup, state, sums, head)

    theta_rows = lax.all_to_all(
        theta_rows, axes, 0, 0, axis_index_groups=[halves[0] + halves[1]], tiled=True
    )

    def index_of():
        t, r, core = (lax.axis_index(a) for a in axes)
        return core * chips + (tgts - 1 - t) * rows + lax.rem(1 + rows - r, rows)

    grad, residual = pl.pallas_call(
        functools.partial(final_body, side, pixels, row_of, index_of),
        out_shape=(
            jax.ShapeDtypeStruct(sup.shape, f32),
            jax.ShapeDtypeStruct(labels.shape, f32),
        ),
        in_specs=[vmem] * 3,
        out_specs=[vmem] * 2,
        scratch_shapes=[pltpu.VMEM((2 * groups, LANE), f32)],
        compiler_params=limit,
        name="final",
    )(theta_rows, planes0, planes1)
    return grad.reshape(support.shape), residual


def solution(mesh):
    tgt, sup = mesh.devices.shape
    chips = Mesh(mesh.devices.reshape(tgt, sup // 2, 2), ("tgt", "row", "core"))
    by_support, by_target = ("row", "core", "tgt"), ("tgt", "row", "core")
    return jax.shard_map(
        local,
        mesh=chips,
        in_specs=(
            P(by_support, None, None),
            P(("row", "core"), None),
            P(by_target, None, None),
            P(by_target, None),
        ),
        out_specs=(P(by_support, None, None), P(by_target, None)),
        check_vma=False,
    )
```
